512 devices in a mesh: fsdp: 32 (over y, z_lo), tp: 16 (over z_hi, x, core).
Axes of the slice: x: 4, y: 4, z: 16 (z_hi: 2, z_lo: 8; z = z_hi * 8 + z_lo), core: 2. Of those that a mesh axis runs over, the one named last changes fastest.
Arguments:
- llm_query: bfloat16 [32, 64, 8192], P('fsdp', None, 'tp'), may hold values from -15 to 15
- llm_kv: bfloat16 [32, 2, 320, 1024], P('fsdp', None, 'tp'), may hold values from -15 to 15
- connector: bfloat16 [8192, 6144], P('tp', 'fsdp'), may hold values from -0.75 to 0.75
- self_query: bfloat16 [32, 2, 1024, 3072], P('fsdp', None, 'tp'), may hold values from -15 to 15
- self_key: bfloat16 [32, 2, 1024, 3072], P('fsdp', None, 'tp'), may hold values from -15 to 15
- latent_value: bfloat16 [32, 2, 1024, 3072], P('fsdp', None, 'tp'), may hold values from -6 to 6
- cotangent: bfloat16 [32, 2, 1024, 3072], P('fsdp', None, 'tp'), may hold values from -6 to 6
Outputs:
- latent_out: bfloat16 [32, 2, 1024, 3072], P('fsdp', None, 'tp')
- self_grad: bfloat16 [32, 2, 1024, 3072], P('fsdp', None, 'tp')
- context_grad: bfloat16 [32, 2, 64, 3072], P('fsdp', None, None, 'tp')
The draws below stay inside these ranges and needn't reach their ends.
All inputs are finite; a program needn't handle non-finite values.
Results may differ from the reference program's by a relative error of at most 0.015.
Values may be sent and summed in bfloat16 or wider, within the bound.
No kernel may reach another device: no remote copies, remote signals or barrier semaphores. Data moves between devices by JAX's collectives and lax.ppermute only.
A program may use at most 128 MiB of HBM per device.

```python
import jax
import jax.numpy as jnp
from jax import lax

HEAD_SIZE = 128
LLM_HEADS = 64
LLM_KV = 8
DENOISER_HEADS = 24
QUERY_TOKENS = 64
LATENT_TOKENS = 1024
SAMPLE_COUNT = 2
PROMPT = 256
LANGUAGE_WIDTH = 8192
DENOISER_WIDTH = 3072
PROMPT_COUNT = 32


def random_base(key, full_shape):
    return jnp.clip(jax.random.normal(key, full_shape, jnp.float32), -6.0, 6.0)


def draw_llm_query(key, part):
    final_output = random_base(jax.random.fold_in(key, 1), (PROMPT_COUNT, QUERY_TOKENS, LLM_HEADS * HEAD_SIZE))
    return final_output.astype(jnp.bfloat16)


def draw_llm_kv(key, part):
    final_output = random_base(jax.random.fold_in(key, 2), (PROMPT_COUNT, 2, PROMPT + QUERY_TOKENS, LLM_KV * HEAD_SIZE))
    return final_output.astype(jnp.bfloat16)


def draw_self_query(key, part):
    final_output = random_base(jax.random.fold_in(key, 3), (PROMPT_COUNT, SAMPLE_COUNT, LATENT_TOKENS, DENOISER_HEADS * HEAD_SIZE))
    return final_output.astype(jnp.bfloat16)


def draw_self_key(key, part):
    final_output = random_base(jax.random.fold_in(key, 4), (PROMPT_COUNT, SAMPLE_COUNT, LATENT_TOKENS, DENOISER_HEADS * HEAD_SIZE))
    return final_output.astype(jnp.bfloat16)


def block_levels(rng, extent, shards, low, high):
    factor_of = 1.0
    for position, blocks in shards:
        heights = jax.random.uniform(jax.random.fold_in(jax.random.fold_in(rng, 6), position), (blocks,), jnp.float32, low / len(shards), high / len(shards))
        factor_of = factor_of * jnp.repeat(jnp.exp(heights), extent[position] // blocks).reshape((-1,) + (1,) * (len(extent) - 1 - position))
    return factor_of


def noise(own_key, shape, width, reach, cuts=(), held_as=jnp.bfloat16):
    values = width * jax.random.normal(own_key, shape, jnp.float32)
    if cuts:
        values = values * block_levels(own_key, shape, cuts, -0.22, 0.18)
    return jnp.clip(values, -reach, reach).astype(held_as)


def setup_inputs(seed: int = 0) -> dict:
    arg_keys = jax.random.split(jax.random.key(seed), 8)
    llm_query = draw_llm_query(jax.random.fold_in(arg_keys[7], 71), 0)
    llm_kv = draw_llm_kv(jax.random.fold_in(arg_keys[7], 71), 0)
    connector = noise(arg_keys[2], (LANGUAGE_WIDTH, 2 * DENOISER_WIDTH), (LANGUAGE_WIDTH // 128) ** -0.5, 0.75, ((0, 16), (1, 32)))
    self_query = draw_self_query(jax.random.fold_in(arg_keys[7], 71), 0)
    self_key = draw_self_key(jax.random.fold_in(arg_keys[7], 71), 0)
    latent_value = noise(arg_keys[5], (PROMPT_COUNT, SAMPLE_COUNT, LATENT_TOKENS, DENOISER_WIDTH), 1.0, 6.0, ((0, 32), (2, 16)))
    cotangent = noise(arg_keys[6], (PROMPT_COUNT, SAMPLE_COUNT, LATENT_TOKENS, DENOISER_WIDTH), 1.0, 6.0, ((0, 32), (2, 16)))
    return dict(llm_query=llm_query, llm_kv=llm_kv, connector=connector, self_query=self_query, self_key=self_key, latent_value=latent_value, cotangent=cotangent)


norm_eps = 1e-06

def softmax_rows(scores, axis_index):
    top_value = lax.optimization_barrier(jnp.max(scores, axis=axis_index, keepdims=True))
    exp_terms = jnp.exp(scores - top_value)
    return exp_terms / lax.optimization_barrier(jnp.sum(exp_terms, axis=axis_index, keepdims=True))

def llm_attention(query_rows, key_value):
    group_size = LLM_HEADS // LLM_KV
    positions = PROMPT + QUERY_TOKENS
    queries = query_rows.reshape(QUERY_TOKENS, LLM_KV, group_size, HEAD_SIZE).astype(jnp.float32)
    keys_all = key_value[0].reshape(positions, LLM_KV, HEAD_SIZE).astype(jnp.float32)
    values_all = key_value[1].reshape(positions, LLM_KV, HEAD_SIZE).astype(jnp.float32)
    scores = jnp.einsum('qkgd,pkd->kgqp', queries, keys_all) * HEAD_SIZE ** (-0.5)
    allowed = jnp.arange(positions)[None, :] <= PROMPT + jnp.arange(QUERY_TOKENS)[:, None]
    scores = jnp.where(allowed, scores, -1e+30)
    weights = softmax_rows(scores, 3).astype(jnp.bfloat16)
    mixed_heads = jnp.einsum('kgqp,pkd->qkgd', weights.astype(jnp.float32), values_all)
    return mixed_heads.astype(jnp.bfloat16).reshape(QUERY_TOKENS, LLM_HEADS * HEAD_SIZE)

def self_item(operands):
    query_item, key_item, value_item = operands
    scores = jnp.dot(query_item, key_item.T, preferred_element_type=jnp.float32) * HEAD_SIZE ** (-0.5)
    weights = softmax_rows(scores, 1).astype(jnp.bfloat16)
    return jnp.dot(weights, value_item, preferred_element_type=jnp.float32).astype(jnp.bfloat16)

def rms_inverse(incoming_values):
    return lax.rsqrt(lax.optimization_barrier(jnp.mean(incoming_values * incoming_values, axis=-1, keepdims=True)) + norm_eps)

def norm_back(grad_normed, normed, inverse):
    return inverse * (grad_normed - normed * lax.optimization_barrier(jnp.mean(grad_normed * normed, axis=-1, keepdims=True)))

def cross_block(latent_heads, condition_tokens, gradient_heads):
    score_scale = HEAD_SIZE ** (-0.5)
    model_width = DENOISER_HEADS * HEAD_SIZE
    condition_keys = condition_tokens[:, :model_width].reshape(QUERY_TOKENS, DENOISER_HEADS, HEAD_SIZE)
    condition_values = condition_tokens[:, model_width:].reshape(QUERY_TOKENS, DENOISER_HEADS, HEAD_SIZE).astype(jnp.float32)
    self_float = latent_heads.astype(jnp.float32)
    query_inverse = rms_inverse(self_float)
    query_normed = self_float * query_inverse
    query_round = query_normed.astype(jnp.bfloat16).astype(jnp.float32)
    key_float = condition_keys.astype(jnp.float32)
    key_inverse = rms_inverse(key_float)
    key_normed = key_float * key_inverse
    key_round = key_normed.astype(jnp.bfloat16).astype(jnp.float32)
    scores = jnp.einsum('hrd,chd->hcr', query_round, key_round) * score_scale
    exp_terms = jnp.exp(scores)
    attention_weights = exp_terms / lax.optimization_barrier(jnp.sum(exp_terms, axis=1, keepdims=True))
    weights_round = attention_weights.astype(jnp.bfloat16).astype(jnp.float32)
    cross_out = jnp.einsum('hcr,chd->hrd', weights_round, condition_values)
    total_heads = self_float + cross_out
    grad_float = gradient_heads.astype(jnp.float32)
    value_gradient = jnp.einsum('hcr,hrd->chd', weights_round, grad_float)
    weight_grad = jnp.einsum('hrd,chd->hcr', grad_float, condition_values)
    delta_rows = lax.optimization_barrier(jnp.sum(attention_weights * weight_grad, axis=1, keepdims=True))
    score_grad = (attention_weights * (weight_grad - delta_rows) * score_scale).astype(jnp.bfloat16).astype(jnp.float32)
    query_grad = jnp.einsum('hcr,chd->hrd', score_grad, key_round)
    key_grad_normed = jnp.einsum('hcr,hrd->chd', score_grad, query_round)
    self_grad = grad_float + norm_back(query_grad, query_normed, query_inverse)
    key_gradient = norm_back(key_grad_normed, key_normed, key_inverse)
    return (total_heads, self_grad, key_gradient, value_gradient)

def one_prompt(connector, operands):
    query_rows, key_value, self_q, self_k, self_v, upstream_gradient = operands
    hidden = llm_attention(query_rows, key_value)
    condition_tokens = jnp.dot(hidden, connector, preferred_element_type=jnp.float32).astype(jnp.bfloat16)

    def to_items(incoming_values):
        return incoming_values.reshape(SAMPLE_COUNT, LATENT_TOKENS, DENOISER_HEADS, HEAD_SIZE).transpose(0, 2, 1, 3).reshape(SAMPLE_COUNT * DENOISER_HEADS, LATENT_TOKENS, HEAD_SIZE)
    latent_attention_output = lax.map(self_item, (to_items(self_q), to_items(self_k), to_items(self_v)))
    gathered_rows = SAMPLE_COUNT * LATENT_TOKENS
    latent_heads = latent_attention_output.reshape(SAMPLE_COUNT, DENOISER_HEADS, LATENT_TOKENS, HEAD_SIZE).transpose(1, 0, 2, 3).reshape(DENOISER_HEADS, gathered_rows, HEAD_SIZE)
    gradient_heads = upstream_gradient.reshape(SAMPLE_COUNT, LATENT_TOKENS, DENOISER_HEADS, HEAD_SIZE).transpose(2, 0, 1, 3).reshape(DENOISER_HEADS, gathered_rows, HEAD_SIZE)
    total_heads, self_grad, key_gradient, value_gradient = cross_block(latent_heads, condition_tokens, gradient_heads)

    def to_rows(incoming_values):
        return incoming_values.reshape(DENOISER_HEADS, SAMPLE_COUNT, LATENT_TOKENS, HEAD_SIZE).transpose(1, 2, 0, 3).reshape(SAMPLE_COUNT, LATENT_TOKENS, DENOISER_HEADS * HEAD_SIZE).astype(jnp.bfloat16)
    gradient_list = jnp.stack([key_gradient.reshape(QUERY_TOKENS, DENOISER_HEADS * HEAD_SIZE), value_gradient.reshape(QUERY_TOKENS, DENOISER_HEADS * HEAD_SIZE)])
    return (to_rows(total_heads), to_rows(self_grad), gradient_list.astype(jnp.bfloat16))

def reference(llm_query, llm_kv, connector, self_query, self_key, latent_value, cotangent):
    latent_out, self_grad, context_grad = lax.map(lambda operands: one_prompt(connector, operands), (llm_query, llm_kv, self_query, self_key, latent_value, cotangent))
    return (latent_out, self_grad, context_grad)
```

```python
import jax
import jax.numpy as jnp
from jax import lax
from jax.experimental import pallas as pl
from jax.sharding import PartitionSpec as P


HEAD_SIZE = 128
QUERY_TOKENS = 64
LATENT_TOKENS = 1024
SAMPLE_COUNT = 2
PROMPT = 256

SCALE = HEAD_SIZE ** (-0.5)
LOG2E = 1.4426950408889634
norm_eps = 1e-06


HALVES = [list(range(8)), list(range(8, 16))]
SWAP_HALF = [(t, (t + 8) % 16) for t in range(16)]
BLOCK = 3 * HEAD_SIZE


def joint(move):
    pairs = []
    for y in range(4):
        for zl in range(8):
            for h in range(2):
                for m in range(4):
                    for c in range(2):
                        y2, zl2, h2, m2, c2 = move(y, zl, h, m, c)
                        source = (8 * y + zl) * 16 + 8 * h + 2 * m + c
                        target = (8 * y2 + zl2) * 16 + 8 * h2 + 2 * m2 + c2
                        pairs.append((source, target))
    return pairs


def head_block(j):
    return 4 * (j % 2) + j // 2


def copy_blocks(*refs):
    *x_refs, o_ref = refs
    at = 0
    for x_ref in x_refs:
        count = x_ref.shape[0]
        o_ref[0, at : at + count] = x_ref[...]
        at += count


def to_blocks(*parts):
    rows = parts[0].shape[1]
    count = sum(x.shape[0] for x in parts)
    return pl.pallas_call(
        copy_blocks,
        grid=(8,),
        in_specs=[pl.BlockSpec((x.shape[0], rows, BLOCK), lambda j: (0, 0, head_block(j))) for x in parts],
        out_specs=pl.BlockSpec((1, count, rows, BLOCK), lambda j: (j, 0, 0, 0)),
        out_shape=jax.ShapeDtypeStruct((8, count, rows, BLOCK), parts[0].dtype),
        name="to_blocks",
    )(*parts)


def copy_rows(x_ref, y_ref, a_ref, b_ref):
    a_ref[0] = x_ref[0, 0]
    a_ref[1] = y_ref[0, 0]
    b_ref[0] = x_ref[0, 1]
    b_ref[1] = y_ref[0, 1]


def from_blocks(x, y):
    rows = x.shape[2]
    in_spec = pl.BlockSpec((1, 2, rows, BLOCK), lambda j: (j, 0, 0, 0))
    out_spec = pl.BlockSpec((SAMPLE_COUNT, rows, BLOCK), lambda j: (0, 0, head_block(j)))
    return pl.pallas_call(
        copy_rows,
        grid=(8,),
        in_specs=[in_spec] * 2,
        out_specs=[out_spec] * 2,
        out_shape=[jax.ShapeDtypeStruct((SAMPLE_COUNT, rows, 8 * BLOCK), x.dtype)] * 2,
        name="from_blocks",
    )(x, y)


def exchange(x):
    return lax.all_to_all(x, "tp", split_axis=0, concat_axis=0, axis_index_groups=HALVES)


def llm_hidden(llm_query, llm_kv):
    half = lax.axis_index("tp") // 8
    rows = llm_kv.shape[2]
    kv = llm_kv[0]
    keep = lax.dynamic_slice_in_dim(kv, half * 512, 512, 2)
    give = lax.dynamic_slice_in_dim(kv, (1 - half) * 512, 512, 2)
    take = lax.ppermute(give, "tp", SWAP_HALF)
    both = jnp.stack([keep, take])
    both = both.reshape(2, 2, rows, 4, HEAD_SIZE).transpose(3, 0, 1, 2, 4)
    both = jnp.broadcast_to(both[:, None], (4, 2, 2, 2, rows, HEAD_SIZE))
    got = exchange(both.reshape(8, 2, 2, rows, HEAD_SIZE))
    keys = got[:, :, 0].reshape(16 * rows, HEAD_SIZE)
    values = got[:, :, 1].reshape(16 * rows, HEAD_SIZE)
    source_half = jnp.stack([half, 1 - half])
    place = jnp.arange(8)[:, None, None] + 8 * source_half[None, :, None]
    position = (place * rows + jnp.arange(rows)[None, None, :]).reshape(1, 16 * rows)
    heads = llm_query.shape[2] // HEAD_SIZE
    queries = llm_query[0].reshape(QUERY_TOKENS * heads, HEAD_SIZE)
    scores = jnp.dot(queries, keys.T, preferred_element_type=jnp.float32) * SCALE
    token = (jnp.arange(QUERY_TOKENS * heads) // heads)[:, None]
    scores = jnp.where(position <= PROMPT + token, scores, -1e30)
    top = jnp.max(scores, axis=1, keepdims=True)
    terms = jnp.exp(scores - top)
    weights = (terms / jnp.sum(terms, axis=1, keepdims=True)).astype(jnp.bfloat16)
    mixed = jnp.dot(weights, values, preferred_element_type=jnp.float32)
    return mixed.astype(jnp.bfloat16).reshape(QUERY_TOKENS, heads * HEAD_SIZE)


def gather_run(connector):
    got = connector[None]
    for k in (4, 2, 1):
        pairs = [(8 * a + b, 8 * a + (b ^ k)) for a in range(4) for b in range(8)]
        got = jnp.concatenate([got, lax.ppermute(got, "fsdp", pairs)])
    return got


def gather_ring(hidden):
    got = [hidden]
    for k in (1, 2, 3):
        pairs = [(8 * a + b, 8 * (a ^ k) + b) for a in range(4) for b in range(8)]
        got.append(lax.ppermute(hidden, "fsdp", pairs))
    return jnp.concatenate(got)


def context_tokens(rows, columns):
    f = lax.axis_index("fsdp")
    y, zl = f // 8, f % 8
    width = columns.shape[2]
    part = jnp.einsum("rk,skn->rsn", rows, columns, preferred_element_type=jnp.float32)
    part = part.astype(jnp.bfloat16).reshape(2, 2, QUERY_TOKENS, 2, 2, 2, width)
    part = part.transpose(5, 4, 1, 0, 3, 2, 6).reshape(8, 2, 2, QUERY_TOKENS, width)
    got = exchange(part)
    mine = jnp.sum(got.astype(jnp.float32), axis=0).astype(jnp.bfloat16)
    there = lax.ppermute(mine, "tp", SWAP_HALF)
    mine = (mine.astype(jnp.float32) + there.astype(jnp.float32)).astype(jnp.bfloat16)
    got = []
    for a in range(2):
        pairs = joint(lambda y, z, h, m, c: (y ^ (2 * a + c), z, h, m ^ (z // 2), y % 2))
        got.append(lax.ppermute(mine[a], ("fsdp", "tp"), pairs))
    one, two = got
    keys = jnp.where(y < 2, one, two)
    values = jnp.where(y < 2, two, one)
    both = jnp.stack([keys, values])
    first = jnp.where(zl % 2 == 0, both[:, 0], both[:, 1])
    second = jnp.where(zl % 2 == 0, both[:, 1], both[:, 0])
    return jnp.concatenate([first, second], axis=2)


def attention_kernel(q_ref, near_ref, far_ref, o_ref):
    half = LATENT_TOKENS // 2
    near_k = near_ref[:, 0].reshape(half, HEAD_SIZE)
    far_k = far_ref[:, 0].reshape(half, HEAD_SIZE)
    near_v = near_ref[:, 1].reshape(half, HEAD_SIZE)
    far_v = far_ref[:, 1].reshape(half, HEAD_SIZE)
    transposed = (((1,), (1,)), ((), ()))
    for part in range(4):
        q = q_ref[2 * part : 2 * part + 2, 0].reshape(half // 4, HEAD_SIZE)
        near = lax.dot_general(q, near_k, transposed, preferred_element_type=jnp.float32)
        far = lax.dot_general(q, far_k, transposed, preferred_element_type=jnp.float32)
        top = jnp.maximum(jnp.max(near, axis=1, keepdims=True), jnp.max(far, axis=1, keepdims=True))
        near = jnp.exp2((near - top) * (SCALE * LOG2E))
        far = jnp.exp2((far - top) * (SCALE * LOG2E))
        total = jnp.sum(near, axis=1, keepdims=True) + jnp.sum(far, axis=1, keepdims=True)
        out = jnp.dot(near.astype(jnp.bfloat16), near_v, preferred_element_type=jnp.float32)
        out += jnp.dot(far.astype(jnp.bfloat16), far_v, preferred_element_type=jnp.float32)
        out = (out / total).astype(jnp.bfloat16)
        o_ref[2 * part : 2 * part + 2] = out.reshape(2, half // 8, HEAD_SIZE)


def attention(sample, query_gradient, near, far):
    rows = near.shape[2]
    pair_spec = pl.BlockSpec((8, 2, rows, HEAD_SIZE), lambda n: (0, 0, 0, n))
    return pl.pallas_call(
        attention_kernel,
        grid=(3,),
        in_specs=[
            pl.BlockSpec((8, 1, rows, HEAD_SIZE), lambda n: (0, sample, 0, n)),
            pair_spec,
            pair_spec,
        ],
        out_specs=pl.BlockSpec((8, rows, HEAD_SIZE), lambda n: (0, 0, n)),
        out_shape=jax.ShapeDtypeStruct((8, rows, BLOCK), jnp.bfloat16),
        name="latent_attention",
    )(query_gradient, near, far)


def cross_kernel(so_ref, g_ref, context_ref, *refs):
    carry_ref = refs[0] if len(refs) == 3 else None
    out_ref, cgrad_ref = refs[-2:]
    half = LATENT_TOKENS // 2
    transposed = (((1,), (1,)), ((), ()))
    first = (((0,), (0,)), ((), ()))
    so = so_ref[...].reshape(half, HEAD_SIZE).astype(jnp.float32)
    g = g_ref[:, 0].reshape(half, HEAD_SIZE)
    ck = context_ref[0].astype(jnp.float32)
    cv = context_ref[1]
    r = lax.rsqrt(jnp.mean(so * so, axis=1, keepdims=True) + norm_eps)
    yq = so * r
    qn = yq.astype(jnp.bfloat16)
    rk = lax.rsqrt(jnp.mean(ck * ck, axis=1, keepdims=True) + norm_eps)
    yk = ck * rk
    kn = yk.astype(jnp.bfloat16)
    scores = lax.dot_general(kn, qn, transposed, preferred_element_type=jnp.float32) * SCALE
    terms = jnp.exp(scores)
    cw = terms / jnp.sum(terms, axis=0, keepdims=True)
    cb = cw.astype(jnp.bfloat16)
    cross = lax.dot_general(cb, cv, first, preferred_element_type=jnp.float32)
    out_ref[:, 0] = (so + cross).astype(jnp.bfloat16).reshape(8, half // 8, HEAD_SIZE)
    dcv = jnp.dot(cb, g, preferred_element_type=jnp.float32)
    dcw = lax.dot_general(cv, g, transposed, preferred_element_type=jnp.float32)
    delta = jnp.sum(cw * dcw, axis=0, keepdims=True)
    ds = (cw * (dcw - delta) * SCALE).astype(jnp.bfloat16)
    dqn = lax.dot_general(ds, kn, first, preferred_element_type=jnp.float32)
    dkn = jnp.dot(ds, qn, preferred_element_type=jnp.float32)
    inner = jnp.mean(dqn * yq, axis=1, keepdims=True)
    grad = g.astype(jnp.float32) + r * (dqn - yq * inner)
    out_ref[:, 1] = grad.astype(jnp.bfloat16).reshape(8, half // 8, HEAD_SIZE)
    if carry_ref is None:
        cgrad_ref[0] = dkn
        cgrad_ref[1] = dcv
    else:
        total = carry_ref[0] + dkn
        along = jnp.mean(total * yk, axis=1, keepdims=True)
        cgrad_ref[0] = (rk * (total - yk * along)).astype(jnp.bfloat16)
        cgrad_ref[1] = (carry_ref[1] + dcv).astype(jnp.bfloat16)


def cross(sample, so, query_gradient, context, carry):
    rows = so.shape[1]
    context_spec = pl.BlockSpec((2, QUERY_TOKENS, HEAD_SIZE), lambda n: (0, 0, n))
    pair_spec = pl.BlockSpec((8, 2, rows, HEAD_SIZE), lambda n: (0, 0, 0, n))
    return pl.pallas_call(
        cross_kernel,
        grid=(3,),
        in_specs=[
            pl.BlockSpec((8, rows, HEAD_SIZE), lambda n: (0, 0, n)),
            pl.BlockSpec((8, 1, rows, HEAD_SIZE), lambda n: (0, 2 + sample, 0, n)),
            context_spec,
        ]
        + [context_spec] * len(carry),
        out_specs=[pair_spec, context_spec],
        out_shape=[
            jax.ShapeDtypeStruct((8, 2, rows, BLOCK), jnp.bfloat16),
            jax.ShapeDtypeStruct(context.shape, jnp.bfloat16 if carry else jnp.float32),
        ],
        name="cross_attention",
    )(so, query_gradient, context, *carry)


def context_gradient(partial):
    half = lax.axis_index("tp") // 8
    width = BLOCK // 2
    low, high = partial[:, :, :width], partial[:, :, width:]
    first = jnp.where(half == 0, low, high)
    second = jnp.where(half == 0, high, low)
    place = lambda h, m, c: 8 * h + 2 * m + c
    coords = [(h, m, c) for h in range(2) for m in range(4) for c in range(2)]
    one = lax.ppermute(first, "tp", [(place(h, m, c), place(c, m, h)) for h, m, c in coords])
    two = lax.ppermute(second, "tp", [(place(h, m, c), place(c, m, 1 - h)) for h, m, c in coords])
    return (one.astype(jnp.float32) + two.astype(jnp.float32)).astype(jnp.bfloat16)[None]


def shards(llm_query, llm_kv, connector, self_query, self_key, latent_value, cotangent):
    return layer(llm_query, llm_kv, connector, self_query[0], self_key[0], latent_value[0], cotangent[0])


def layer(llm_query, llm_kv, connector, query, key, value, cotangent):
    near, far = [], []
    for s in range(SAMPLE_COUNT):
        near.append(exchange(to_blocks(key[s : s + 1], value[s : s + 1])))
        far.append(lax.ppermute(near[s], "tp", SWAP_HALF))
    columns = gather_run(connector)
    hidden = llm_hidden(llm_query, llm_kv)
    query_gradient = exchange(to_blocks(query, cotangent))
    context = context_tokens(gather_ring(hidden), columns)
    out, carry = [], ()
    for s in range(SAMPLE_COUNT):
        so = attention(s, query_gradient, near[s], far[s])
        result, partial = cross(s, so, query_gradient, context, carry)
        carry = (partial,)
        out.append(exchange(result))
    context_grad = context_gradient(partial)
    latent_out, self_grad = from_blocks(*out)
    return (latent_out[None], self_grad[None], context_grad)


def solution(mesh):
    placed = (
        P("fsdp", None, "tp"),
        P("fsdp", None, "tp", None),
        P("tp", "fsdp"),
        P("fsdp", None, "tp", None),
        P("fsdp", None, "tp", None),
        P("fsdp", None, "tp", None),
        P("fsdp", None, "tp", None),
    )
    return jax.shard_map(
        shards,
        mesh=mesh,
        in_specs=placed,
        out_specs=(
            P("fsdp", None, "tp", None),
            P("fsdp", None, "tp", None),
            P("fsdp", None, None, "tp"),
        ),
        check_vma=False,
    )
```

```python
import jax
import jax.numpy as jnp
from jax import lax
from jax.experimental import pallas as pl
from jax.sharding import PartitionSpec as P


HEAD_SIZE = 128
QUERY_TOKENS = 64
LATENT_TOKENS = 1024
SAMPLE_COUNT = 2
PROMPT = 256

SCALE = HEAD_SIZE ** (-0.5)
LOG2E = 1.4426950408889634
norm_eps = 1e-06


HALVES = [list(range(8)), list(range(8, 16))]
SWAP_HALF = [(t, (t + 8) % 16) for t in range(16)]
BLOCK = 3 * HEAD_SIZE


def joint(move):
    pairs = []
    for y in range(4):
        for zl in range(8):
            for h in range(2):
                for m in range(4):
                    for c in range(2):
                        y2, zl2, h2, m2, c2 = move(y, zl, h, m, c)
                        source = (8 * y + zl) * 16 + 8 * h + 2 * m + c
                        target = (8 * y2 + zl2) * 16 + 8 * h2 + 2 * m2 + c2
                        pairs.append((source, target))
    return pairs


def copy_blocks(*refs):
    *x_refs, o_ref = refs
    at = 0
    for x_ref in x_refs:
        count = x_ref.shape[0]
        for m in range(4):
            o_ref[m, 0, at : at + count] = x_ref[:, :, BLOCK * m : BLOCK * (m + 1)]
        at += count


def to_blocks(first, count, *parts):
    rows = parts[0].shape[1]
    total = count * len(parts)
    out = pl.pallas_call(
        copy_blocks,
        grid=(2,),
        in_specs=[pl.BlockSpec((count, rows, 4 * BLOCK), lambda c: (first, 0, c))] * len(parts),
        out_specs=pl.BlockSpec((4, 1, total, rows, BLOCK), lambda c: (0, c, 0, 0, 0)),
        out_shape=jax.ShapeDtypeStruct((4, 2, total, rows, BLOCK), parts[0].dtype),
        name="to_blocks",
    )(*parts)
    return out.reshape(8, total, rows, BLOCK)


def copy_rows(*refs):
    *in_refs, a_ref, b_ref = refs
    for s, x_ref in enumerate(in_refs):
        for m in range(4):
            a_ref[s, :, BLOCK * m : BLOCK * (m + 1)] = x_ref[m, 0, 0]
            b_ref[s, :, BLOCK * m : BLOCK * (m + 1)] = x_ref[m, 0, 1]


def from_blocks(*parts):
    rows = parts[0].shape[2]
    return pl.pallas_call(
        copy_rows,
        grid=(2,),
        in_specs=[pl.BlockSpec((4, 1, 2, rows, BLOCK), lambda c: (0, c, 0, 0, 0))] * SAMPLE_COUNT,
        out_specs=[pl.BlockSpec((SAMPLE_COUNT, rows, 4 * BLOCK), lambda c: (0, 0, c))] * 2,
        out_shape=[jax.ShapeDtypeStruct((SAMPLE_COUNT, rows, 8 * BLOCK), parts[0].dtype)] * 2,
        name="from_blocks",
    )(*(x.reshape(4, 2, 2, rows, BLOCK) for x in parts))


def exchange(x):
    return lax.all_to_all(x, "tp", split_axis=0, concat_axis=0, axis_index_groups=HALVES)


def llm_hidden(llm_query, llm_kv):
    half = lax.axis_index("tp") // 8
    rows = llm_kv.shape[2]
    kv = llm_kv[0]
    keep = lax.dynamic_slice_in_dim(kv, half * 512, 512, 2)
    give = lax.dynamic_slice_in_dim(kv, (1 - half) * 512, 512, 2)
    take = lax.ppermute(give, "tp", SWAP_HALF)
    both = jnp.stack([keep, take])
    both = both.reshape(2, 2, rows, 4, HEAD_SIZE).transpose(3, 0, 1, 2, 4)
    both = jnp.broadcast_to(both[:, None], (4, 2, 2, 2, rows, HEAD_SIZE))
    got = exchange(both.reshape(8, 2, 2, rows, HEAD_SIZE))
    keys = got[:, :, 0].reshape(16 * rows, HEAD_SIZE)
    values = got[:, :, 1].reshape(16 * rows, HEAD_SIZE)
    source_half = jnp.stack([half, 1 - half])
    place = jnp.arange(8)[:, None, None] + 8 * source_half[None, :, None]
    position = (place * rows + jnp.arange(rows)[None, None, :]).reshape(1, 16 * rows)
    heads = llm_query.shape[2] // HEAD_SIZE
    queries = llm_query[0].reshape(QUERY_TOKENS * heads, HEAD_SIZE)
    scores = jnp.dot(queries, keys.T, preferred_element_type=jnp.float32) * SCALE
    token = (jnp.arange(QUERY_TOKENS * heads) // heads)[:, None]
    scores = jnp.where(position <= PROMPT + token, scores, -1e30)
    top = jnp.max(scores, axis=1, keepdims=True)
    terms = jnp.exp(scores - top)
    weights = (terms / jnp.sum(terms, axis=1, keepdims=True)).astype(jnp.bfloat16)
    mixed = jnp.dot(weights, values, preferred_element_type=jnp.float32)
    return mixed.astype(jnp.bfloat16).reshape(QUERY_TOKENS, heads * HEAD_SIZE)


def gather_run(connector):
    got = connector[None]
    for k in (4, 2, 1):
        pairs = [(8 * a + b, 8 * a + (b ^ k)) for a in range(4) for b in range(8)]
        got = jnp.concatenate([got, lax.ppermute(got, "fsdp", pairs)])
    return got


def gather_ring(hidden):
    got = [hidden]
    for k in (1, 2, 3):
        pairs = [(8 * a + b, 8 * (a ^ k) + b) for a in range(4) for b in range(8)]
        got.append(lax.ppermute(hidden, "fsdp", pairs))
    return jnp.concatenate(got)


def context_tokens(rows, columns):
    f = lax.axis_index("fsdp")
    y, zl = f // 8, f % 8
    width = columns.shape[2]
    part = jnp.einsum("rk,skn->rsn", rows, columns, preferred_element_type=jnp.float32)
    part = part.astype(jnp.bfloat16).reshape(2, 2, QUERY_TOKENS, 2, 2, 2, width)
    part = part.transpose(5, 4, 1, 0, 3, 2, 6).reshape(8, 2, 2, QUERY_TOKENS, width)
    got = exchange(part)
    mine = jnp.sum(got.astype(jnp.float32), axis=0).astype(jnp.bfloat16)
    there = lax.ppermute(mine, "tp", SWAP_HALF)
    mine = (mine.astype(jnp.float32) + there.astype(jnp.float32)).astype(jnp.bfloat16)
    got = []
    for a in range(2):
        pairs = joint(lambda y, z, h, m, c: (y ^ (2 * a + c), z, h, m ^ (z // 2), y % 2))
        got.append(lax.ppermute(mine[a], ("fsdp", "tp"), pairs))
    one, two = got
    keys = jnp.where(y < 2, one, two)
    values = jnp.where(y < 2, two, one)
    both = jnp.stack([keys, values])
    first = jnp.where(zl % 2 == 0, both[:, 0], both[:, 1])
    second = jnp.where(zl % 2 == 0, both[:, 1], both[:, 0])
    return jnp.concatenate([first, second], axis=2)


def attention_kernel(q_ref, near_ref, far_ref, o_ref):
    half = LATENT_TOKENS // 2
    near_k = near_ref[:, 0].reshape(half, HEAD_SIZE)
    far_k = far_ref[:, 0].reshape(half, HEAD_SIZE)
    near_v = near_ref[:, 1].reshape(half, HEAD_SIZE)
    far_v = far_ref[:, 1].reshape(half, HEAD_SIZE)
    transposed = (((1,), (1,)), ((), ()))
    for part in range(4):
        q = q_ref[2 * part : 2 * part + 2, 0].reshape(half // 4, HEAD_SIZE)
        near = lax.dot_general(q, near_k, transposed, preferred_element_type=jnp.float32)
        far = lax.dot_general(q, far_k, transposed, preferred_element_type=jnp.float32)
        top = jnp.maximum(jnp.max(near, axis=1, keepdims=True), jnp.max(far, axis=1, keepdims=True))
        near = jnp.exp2((near - top) * (SCALE * LOG2E))
        far = jnp.exp2((far - top) * (SCALE * LOG2E))
        total = jnp.sum(near, axis=1, keepdims=True) + jnp.sum(far, axis=1, keepdims=True)
        out = jnp.dot(near.astype(jnp.bfloat16), near_v, preferred_element_type=jnp.float32)
        out += jnp.dot(far.astype(jnp.bfloat16), far_v, preferred_element_type=jnp.float32)
        out = (out / total).astype(jnp.bfloat16)
        o_ref[2 * part : 2 * part + 2] = out.reshape(2, half // 8, HEAD_SIZE)


def attention(sample, query_gradient, near, far):
    rows = near.shape[2]
    pair_spec = pl.BlockSpec((8, 2, rows, HEAD_SIZE), lambda n: (0, 0, 0, n))
    return pl.pallas_call(
        attention_kernel,
        grid=(3,),
        in_specs=[
            pl.BlockSpec((8, 1, rows, HEAD_SIZE), lambda n: (0, sample, 0, n)),
            pair_spec,
            pair_spec,
        ],
        out_specs=pl.BlockSpec((8, rows, HEAD_SIZE), lambda n: (0, 0, n)),
        out_shape=jax.ShapeDtypeStruct((8, rows, BLOCK), jnp.bfloat16),
        name="latent_attention",
    )(query_gradient, near, far)


def cross_kernel(so_ref, g_ref, context_ref, *refs):
    carry_ref = refs[0] if len(refs) == 3 else None
    out_ref, cgrad_ref = refs[-2:]
    half = LATENT_TOKENS // 2
    transposed = (((1,), (1,)), ((), ()))
    first = (((0,), (0,)), ((), ()))
    so = so_ref[...].reshape(half, HEAD_SIZE).astype(jnp.float32)
    g = g_ref[:, 0].reshape(half, HEAD_SIZE)
    ck = context_ref[0].astype(jnp.float32)
    cv = context_ref[1]
    r = lax.rsqrt(jnp.mean(so * so, axis=1, keepdims=True) + norm_eps)
    yq = so * r
    qn = yq.astype(jnp.bfloat16)
    rk = lax.rsqrt(jnp.mean(ck * ck, axis=1, keepdims=True) + norm_eps)
    yk = ck * rk
    kn = yk.astype(jnp.bfloat16)
    scores = lax.dot_general(kn, qn, transposed, preferred_element_type=jnp.float32) * SCALE
    terms = jnp.exp(scores)
    cw = terms / jnp.sum(terms, axis=0, keepdims=True)
    cb = cw.astype(jnp.bfloat16)
    cross = lax.dot_general(cb, cv, first, preferred_element_type=jnp.float32)
    out_ref[:, 0] = (so + cross).astype(jnp.bfloat16).reshape(8, half // 8, HEAD_SIZE)
    dcv = jnp.dot(cb, g, preferred_element_type=jnp.float32)
    dcw = lax.dot_general(cv, g, transposed, preferred_element_type=jnp.float32)
    delta = jnp.sum(cw * dcw, axis=0, keepdims=True)
    ds = (cw * (dcw - delta) * SCALE).astype(jnp.bfloat16)
    dqn = lax.dot_general(ds, kn, first, preferred_element_type=jnp.float32)
    dkn = jnp.dot(ds, qn, preferred_element_type=jnp.float32)
    inner = jnp.mean(dqn * yq, axis=1, keepdims=True)
    grad = g.astype(jnp.float32) + r * (dqn - yq * inner)
    out_ref[:, 1] = grad.astype(jnp.bfloat16).reshape(8, half // 8, HEAD_SIZE)
    if carry_ref is None:
        cgrad_ref[0] = dkn
        cgrad_ref[1] = dcv
    else:
        total = carry_ref[0] + dkn
        along = jnp.mean(total * yk, axis=1, keepdims=True)
        cgrad_ref[0] = (rk * (total - yk * along)).astype(jnp.bfloat16)
        cgrad_ref[1] = (carry_ref[1] + dcv).astype(jnp.bfloat16)


def cross(sample, so, query_gradient, context, carry):
    rows = so.shape[1]
    context_spec = pl.BlockSpec((2, QUERY_TOKENS, HEAD_SIZE), lambda n: (0, 0, n))
    pair_spec = pl.BlockSpec((8, 2, rows, HEAD_SIZE), lambda n: (0, 0, 0, n))
    return pl.pallas_call(
        cross_kernel,
        grid=(3,),
        in_specs=[
            pl.BlockSpec((8, rows, HEAD_SIZE), lambda n: (0, 0, n)),
            pl.BlockSpec((8, 1, rows, HEAD_SIZE), lambda n: (0, 2 + sample, 0, n)),
            context_spec,
        ]
        + [context_spec] * len(carry),
        out_specs=[pair_spec, context_spec],
        out_shape=[
            jax.ShapeDtypeStruct((8, 2, rows, BLOCK), jnp.bfloat16),
            jax.ShapeDtypeStruct(context.shape, jnp.bfloat16 if carry else jnp.float32),
        ],
        name="cross_attention",
    )(so, query_gradient, context, *carry)


def context_gradient(partial):
    half = lax.axis_index("tp") // 8
    width = BLOCK // 2
    low, high = partial[:, :, :width], partial[:, :, width:]
    first = jnp.where(half == 0, low, high)
    second = jnp.where(half == 0, high, low)
    place = lambda h, m, c: 8 * h + 2 * m + c
    coords = [(h, m, c) for h in range(2) for m in range(4) for c in range(2)]
    one = lax.ppermute(first, "tp", [(place(h, m, c), place(c, m, h)) for h, m, c in coords])
    two = lax.ppermute(second, "tp", [(place(h, m, c), place(c, m, 1 - h)) for h, m, c in coords])
    return (one.astype(jnp.float32) + two.astype(jnp.float32)).astype(jnp.bfloat16)[None]


def shards(llm_query, llm_kv, connector, self_query, self_key, latent_value, cotangent):
    return layer(llm_query, llm_kv, connector, self_query[0], self_key[0], latent_value[0], cotangent[0])


def layer(llm_query, llm_kv, connector, query, key, value, cotangent):
    near, far = [], []
    for s in range(SAMPLE_COUNT):
        near.append(exchange(to_blocks(s, 1, key, value)))
        far.append(lax.ppermute(near[s], "tp", SWAP_HALF))
    columns = gather_run(connector)
    hidden = llm_hidden(llm_query, llm_kv)
    query_gradient = exchange(to_blocks(0, 2, query, cotangent))
    context = context_tokens(gather_ring(hidden), columns)
    out, carry = [], ()
    for s in range(SAMPLE_COUNT):
        so = attention(s, query_gradient, near[s], far[s])
        result, partial = cross(s, so, query_gradient, context, carry)
        carry = (partial,)
        out.append(exchange(result))
    context_grad = context_gradient(partial)
    latent_out, self_grad = from_blocks(*out)
    return (latent_out[None], self_grad[None], context_grad)


def solution(mesh):
    placed = (
        P("fsdp", None, "tp"),
        P("fsdp", None, "tp", None),
        P("tp", "fsdp"),
        P("fsdp", None, "tp", None),
        P("fsdp", None, "tp", None),
        P("fsdp", None, "tp", None),
        P("fsdp", None, "tp", None),
    )
    return jax.shard_map(
        shards,
        mesh=mesh,
        in_specs=placed,
        out_specs=(
            P("fsdp", None, "tp", None),
            P("fsdp", None, "tp", None),
            P("fsdp", None, None, "tp"),
        ),
        check_vma=False,
    )
```

```python
import jax
import jax.numpy as jnp
from jax import lax
from jax.experimental import pallas as pl
from jax.sharding import PartitionSpec as P


HEAD_SIZE = 128
QUERY_TOKENS = 64
LATENT_TOKENS = 1024
SAMPLE_COUNT = 2
PROMPT = 256

SCALE = HEAD_SIZE ** (-0.5)
LOG2E = 1.4426950408889634
norm_eps = 1e-06


HALVES = [list(range(8)), list(range(8, 16))]
SWAP_HALF = [(t, (t + 8) % 16) for t in range(16)]
BLOCK = 3 * HEAD_SIZE


def joint(move):
    pairs = []
    for y in range(4):
        for zl in range(8):
            for h in range(2):
                for m in range(4):
                    for c in range(2):
                        y2, zl2, h2, m2, c2 = move(y, zl, h, m, c)
                        source = (8 * y + zl) * 16 + 8 * h + 2 * m + c
                        target = (8 * y2 + zl2) * 16 + 8 * h2 + 2 * m2 + c2
                        pairs.append((source, target))
    return pairs


def copy_blocks(*refs):
    *x_refs, o_ref = refs
    at = 0
    for x_ref in x_refs:
        count = x_ref.shape[0]
        for m in range(4):
            o_ref[m, 0, at : at + count] = x_ref[:, :, BLOCK * m : BLOCK * (m + 1)]
        at += count


def to_blocks(first, count, *parts):
    rows = parts[0].shape[1]
    total = count * len(parts)
    out = pl.pallas_call(
        copy_blocks,
        grid=(2,),
        in_specs=[pl.BlockSpec((count, rows, 4 * BLOCK), lambda c: (first, 0, c))] * len(parts),
        out_specs=pl.BlockSpec((4, 1, total, rows, BLOCK), lambda c: (0, c, 0, 0, 0)),
        out_shape=jax.ShapeDtypeStruct((4, 2, total, rows, BLOCK), parts[0].dtype),
        name="to_blocks",
    )(*parts)
    return out.reshape(8, total, rows, BLOCK)


def copy_rows(*refs):
    *in_refs, a_ref, b_ref = refs
    for s, x_ref in enumerate(in_refs):
        for m in range(4):
            a_ref[s, :, BLOCK * m : BLOCK * (m + 1)] = x_ref[m, 0, 0]
            b_ref[s, :, BLOCK * m : BLOCK * (m + 1)] = x_ref[m, 0, 1]


def from_blocks(*parts):
    rows = parts[0].shape[2]
    return pl.pallas_call(
        copy_rows,
        grid=(2,),
        in_specs=[pl.BlockSpec((4, 1, 2, rows, BLOCK), lambda c: (0, c, 0, 0, 0))] * SAMPLE_COUNT,
        out_specs=[pl.BlockSpec((SAMPLE_COUNT, rows, 4 * BLOCK), lambda c: (0, 0, c))] * 2,
        out_shape=[jax.ShapeDtypeStruct((SAMPLE_COUNT, rows, 8 * BLOCK), parts[0].dtype)] * 2,
        name="from_blocks",
    )(*(x.reshape(4, 2, 2, rows, BLOCK) for x in parts))


def exchange(x):
    return lax.all_to_all(x, "tp", split_axis=0, concat_axis=0, axis_index_groups=HALVES)


def llm_hidden(llm_query, llm_kv):
    half = lax.axis_index("tp") // 8
    rows = llm_kv.shape[2]
    kv = llm_kv[0]
    keep = lax.dynamic_slice_in_dim(kv, half * 512, 512, 2)
    give = lax.dynamic_slice_in_dim(kv, (1 - half) * 512, 512, 2)
    take = lax.ppermute(give, "tp", SWAP_HALF)
    both = jnp.stack([keep, take])
    both = both.reshape(2, 2, rows, 4, HEAD_SIZE).transpose(3, 0, 1, 2, 4)
    both = jnp.broadcast_to(both[:, None], (4, 2, 2, 2, rows, HEAD_SIZE))
    got = exchange(both.reshape(8, 2, 2, rows, HEAD_SIZE))
    keys = got[:, :, 0].reshape(16 * rows, HEAD_SIZE)
    values = got[:, :, 1].reshape(16 * rows, HEAD_SIZE)
    source_half = jnp.stack([half, 1 - half])
    place = jnp.arange(8)[:, None, None] + 8 * source_half[None, :, None]
    position = (place * rows + jnp.arange(rows)[None, None, :]).reshape(1, 16 * rows)
    heads = llm_query.shape[2] // HEAD_SIZE
    queries = llm_query[0].reshape(QUERY_TOKENS * heads, HEAD_SIZE)
    scores = jnp.dot(queries, keys.T, preferred_element_type=jnp.float32) * SCALE
    token = (jnp.arange(QUERY_TOKENS * heads) // heads)[:, None]
    scores = jnp.where(position <= PROMPT + token, scores, -1e30)
    top = jnp.max(scores, axis=1, keepdims=True)
    terms = jnp.exp(scores - top)
    weights = (terms / jnp.sum(terms, axis=1, keepdims=True)).astype(jnp.bfloat16)
    mixed = jnp.dot(weights, values, preferred_element_type=jnp.float32)
    return mixed.astype(jnp.bfloat16).reshape(QUERY_TOKENS, heads * HEAD_SIZE)


def gather_columns(connector):
    got = connector[None]
    for k in (2, 1):
        pairs = [(8 * a + b, 8 * a + (b ^ k)) for a in range(4) for b in range(8)]
        got = jnp.concatenate([got, lax.ppermute(got, "fsdp", pairs)])
    return got


def gather_rows(hidden):
    pairs = [(8 * a + b, 8 * a + (b ^ 4)) for a in range(4) for b in range(8)]
    got = [jnp.concatenate([hidden, lax.ppermute(hidden, "fsdp", pairs)])]
    for k in (1, 2, 3):
        pairs = [(8 * a + b, 8 * (a ^ k) + b) for a in range(4) for b in range(8)]
        got.append(lax.ppermute(got[0], "fsdp", pairs))
    return jnp.concatenate(got)


def context_tokens(rows, columns):
    f = lax.axis_index("fsdp")
    y, zl = f // 8, f % 8
    width = columns.shape[2]
    part = jnp.einsum("rk,skn->rsn", rows, columns, preferred_element_type=jnp.float32)
    part = part.astype(jnp.bfloat16).reshape(2, 2, 2, QUERY_TOKENS, 2, 2, width)
    part = part.transpose(2, 5, 1, 0, 4, 3, 6).reshape(8, 2, 2, QUERY_TOKENS, width)
    got = exchange(part)
    mine = jnp.sum(got.astype(jnp.float32), axis=0).astype(jnp.bfloat16)
    there = lax.ppermute(mine, "tp", SWAP_HALF)
    mine = (mine.astype(jnp.float32) + there.astype(jnp.float32)).astype(jnp.bfloat16)
    got = []
    for a in range(2):
        pairs = joint(
            lambda y, z, h, m, c: (
                y ^ (2 * a + c),
                z ^ (4 * (m // 2)),
                h,
                2 * (z // 4) + (z // 2 % 2 ^ m % 2),
                y % 2,
            )
        )
        got.append(lax.ppermute(mine[a], ("fsdp", "tp"), pairs))
    one, two = got
    keys = jnp.where(y < 2, one, two)
    values = jnp.where(y < 2, two, one)
    both = jnp.stack([keys, values])
    first = jnp.where(zl % 2 == 0, both[:, 0], both[:, 1])
    second = jnp.where(zl % 2 == 0, both[:, 1], both[:, 0])
    return jnp.concatenate([first, second], axis=2)


def attention_kernel(q_ref, near_ref, fk_ref, fv_ref, o_ref):
    half = LATENT_TOKENS // 2
    near_k = near_ref[:, 0].reshape(half, HEAD_SIZE)
    far_k = fk_ref[...].reshape(half, HEAD_SIZE)
    near_v = near_ref[:, 1].reshape(half, HEAD_SIZE)
    far_v = fv_ref[...].reshape(half, HEAD_SIZE)
    transposed = (((1,), (1,)), ((), ()))
    for part in range(4):
        q = q_ref[2 * part : 2 * part + 2, 0].reshape(half // 4, HEAD_SIZE)
        near = lax.dot_general(q, near_k, transposed, preferred_element_type=jnp.float32)
        far = lax.dot_general(q, far_k, transposed, preferred_element_type=jnp.float32)
        top = jnp.maximum(jnp.max(near, axis=1, keepdims=True), jnp.max(far, axis=1, keepdims=True))
        near = jnp.exp2((near - top) * (SCALE * LOG2E))
        far = jnp.exp2((far - top) * (SCALE * LOG2E))
        total = jnp.sum(near, axis=1, keepdims=True) + jnp.sum(far, axis=1, keepdims=True)
        out = jnp.dot(near.astype(jnp.bfloat16), near_v, preferred_element_type=jnp.float32)
        out += jnp.dot(far.astype(jnp.bfloat16), far_v, preferred_element_type=jnp.float32)
        out = (out / total).astype(jnp.bfloat16)
        o_ref[2 * part : 2 * part + 2] = out.reshape(2, half // 8, HEAD_SIZE)


def attention(sample, query_gradient, near, far_k, far_v):
    rows = near.shape[2]
    spec = pl.BlockSpec((8, rows, HEAD_SIZE), lambda n: (0, 0, n))
    return pl.pallas_call(
        attention_kernel,
        grid=(3,),
        in_specs=[
            pl.BlockSpec((8, 1, rows, HEAD_SIZE), lambda n: (0, sample, 0, n)),
            pl.BlockSpec((8, 2, rows, HEAD_SIZE), lambda n: (0, 0, 0, n)),
            spec,
            spec,
        ],
        out_specs=spec,
        out_shape=jax.ShapeDtypeStruct((8, rows, BLOCK), jnp.bfloat16),
        name="latent_attention",
    )(query_gradient, near, far_k, far_v)


def cross_kernel(so_ref, g_ref, context_ref, *refs):
    carry_ref = refs[0] if len(refs) == 3 else None
    out_ref, cgrad_ref = refs[-2:]
    half = LATENT_TOKENS // 2
    transposed = (((1,), (1,)), ((), ()))
    first = (((0,), (0,)), ((), ()))
    so = so_ref[...].reshape(half, HEAD_SIZE).astype(jnp.float32)
    g = g_ref[:, 0].reshape(half, HEAD_SIZE)
    ck = context_ref[0].astype(jnp.float32)
    cv = context_ref[1]
    r = lax.rsqrt(jnp.mean(so * so, axis=1, keepdims=True) + norm_eps)
    yq = so * r
    qn = yq.astype(jnp.bfloat16)
    rk = lax.rsqrt(jnp.mean(ck * ck, axis=1, keepdims=True) + norm_eps)
    yk = ck * rk
    kn = yk.astype(jnp.bfloat16)
    scores = lax.dot_general(kn, qn, transposed, preferred_element_type=jnp.float32) * SCALE
    terms = jnp.exp(scores)
    cw = terms / jnp.sum(terms, axis=0, keepdims=True)
    cb = cw.astype(jnp.bfloat16)
    cross = lax.dot_general(cb, cv, first, preferred_element_type=jnp.float32)
    out_ref[:, 0] = (so + cross).astype(jnp.bfloat16).reshape(8, half // 8, HEAD_SIZE)
    dcv = jnp.dot(cb, g, preferred_element_type=jnp.float32)
    dcw = lax.dot_general(cv, g, transposed, preferred_element_type=jnp.float32)
    delta = jnp.sum(cw * dcw, axis=0, keepdims=True)
    ds = (cw * (dcw - delta) * SCALE).astype(jnp.bfloat16)
    dqn = lax.dot_general(ds, kn, first, preferred_element_type=jnp.float32)
    dkn = jnp.dot(ds, qn, preferred_element_type=jnp.float32)
    inner = jnp.mean(dqn * yq, axis=1, keepdims=True)
    grad = g.astype(jnp.float32) + r * (dqn - yq * inner)
    out_ref[:, 1] = grad.astype(jnp.bfloat16).reshape(8, half // 8, HEAD_SIZE)
    if carry_ref is None:
        cgrad_ref[0] = dkn
        cgrad_ref[1] = dcv
    else:
        total = carry_ref[0] + dkn
        along = jnp.mean(total * yk, axis=1, keepdims=True)
        cgrad_ref[0] = (rk * (total - yk * along)).astype(jnp.bfloat16)
        cgrad_ref[1] = (carry_ref[1] + dcv).astype(jnp.bfloat16)


def cross(sample, so, query_gradient, context, carry):
    rows = so.shape[1]
    context_spec = pl.BlockSpec((2, QUERY_TOKENS, HEAD_SIZE), lambda n: (0, 0, n))
    pair_spec = pl.BlockSpec((8, 2, rows, HEAD_SIZE), lambda n: (0, 0, 0, n))
    return pl.pallas_call(
        cross_kernel,
        grid=(3,),
        in_specs=[
            pl.BlockSpec((8, rows, HEAD_SIZE), lambda n: (0, 0, n)),
            pl.BlockSpec((8, 1, rows, HEAD_SIZE), lambda n: (0, 2 + sample, 0, n)),
            context_spec,
        ]
        + [context_spec] * len(carry),
        out_specs=[pair_spec, context_spec],
        out_shape=[
            jax.ShapeDtypeStruct((8, 2, rows, BLOCK), jnp.bfloat16),
            jax.ShapeDtypeStruct(context.shape, jnp.bfloat16 if carry else jnp.float32),
        ],
        name="cross_attention",
    )(so, query_gradient, context, *carry)


def context_gradient(partial):
    half = lax.axis_index("tp") // 8
    width = BLOCK // 2
    low, high = partial[:, :, :width], partial[:, :, width:]
    first = jnp.where(half == 0, low, high)
    second = jnp.where(half == 0, high, low)
    place = lambda h, m, c: 8 * h + 2 * m + c
    coords = [(h, m, c) for h in range(2) for m in range(4) for c in range(2)]
    one = lax.ppermute(first, "tp", [(place(h, m, c), place(c, m, h)) for h, m, c in coords])
    two = lax.ppermute(second, "tp", [(place(h, m, c), place(c, m, 1 - h)) for h, m, c in coords])
    return (one.astype(jnp.float32) + two.astype(jnp.float32)).astype(jnp.bfloat16)[None]


def shards(llm_query, llm_kv, connector, self_query, self_key, latent_value, cotangent):
    return layer(llm_query, llm_kv, connector, self_query[0], self_key[0], latent_value[0], cotangent[0])


def layer(llm_query, llm_kv, connector, query, key, value, cotangent):
    near, far = [], []
    for s in range(SAMPLE_COUNT):
        near.append(exchange(to_blocks(s, 1, key, value)))
        far.append([lax.ppermute(near[s][:, i], "tp", SWAP_HALF) for i in range(2)])
    columns = gather_columns(connector)
    hidden = llm_hidden(llm_query, llm_kv)
    query_gradient = exchange(to_blocks(0, 2, query, cotangent))
    context = context_tokens(gather_rows(hidden), columns)
    out, carry = [], ()
    for s in range(SAMPLE_COUNT):
        so = attention(s, query_gradient, near[s], *far[s])
        result, partial = cross(s, so, query_gradient, context, carry)
        carry = (partial,)
        out.append(exchange(result))
    context_grad = context_gradient(partial)
    latent_out, self_grad = from_blocks(*out)
    return (latent_out[None], self_grad[None], context_grad)


def solution(mesh):
    placed = (
        P("fsdp", None, "tp"),
        P("fsdp", None, "tp", None),
        P("tp", "fsdp"),
        P("fsdp", None, "tp", None),
        P("fsdp", None, "tp", None),
        P("fsdp", None, "tp", None),
        P("fsdp", None, "tp", None),
    )
    return jax.shard_map(
        shards,
        mesh=mesh,
        in_specs=placed,
        out_specs=(
            P("fsdp", None, "tp", None),
            P("fsdp", None, "tp", None),
            P("fsdp", None, None, "tp"),
        ),
        check_vma=False,
    )
```

```python
import jax
import jax.numpy as jnp
from jax import lax
from jax.experimental import pallas as pl
from jax.sharding import PartitionSpec as P


HEAD_SIZE = 128
QUERY_TOKENS = 64
LATENT_TOKENS = 1024
SAMPLE_COUNT = 2
PROMPT = 256

SCALE = HEAD_SIZE ** (-0.5)
LOG2E = 1.4426950408889634
norm_eps = 1e-06


HALVES = [list(range(8)), list(range(8, 16))]
SWAP_HALF = [(t, (t + 8) % 16) for t in range(16)]
BLOCK = 3 * HEAD_SIZE


def joint(move):
    pairs = []
    for y in range(4):
        for zl in range(8):
            for h in range(2):
                for m in range(4):
                    for c in range(2):
                        y2, zl2, h2, m2, c2 = move(y, zl, h, m, c)
                        source = (8 * y + zl) * 16 + 8 * h + 2 * m + c
                        target = (8 * y2 + zl2) * 16 + 8 * h2 + 2 * m2 + c2
                        pairs.append((source, target))
    return pairs


def copy_blocks(*refs):
    *x_refs, o_ref = refs
    at = 0
    for x_ref in x_refs:
        count = x_ref.shape[0]
        for m in range(4):
            o_ref[m, 0, at : at + count] = x_ref[:, :, BLOCK * m : BLOCK * (m + 1)]
        at += count


def to_blocks(first, count, *parts):
    rows = parts[0].shape[1]
    total = count * len(parts)
    out = pl.pallas_call(
        copy_blocks,
        grid=(2,),
        in_specs=[pl.BlockSpec((count, rows, 4 * BLOCK), lambda c: (first, 0, c))] * len(parts),
        out_specs=pl.BlockSpec((4, 1, total, rows, BLOCK), lambda c: (0, c, 0, 0, 0)),
        out_shape=jax.ShapeDtypeStruct((4, 2, total, rows, BLOCK), parts[0].dtype),
        name="to_blocks",
    )(*parts)
    return out.reshape(8, total, rows, BLOCK)


def copy_rows(*refs):
    *in_refs, a_ref, b_ref = refs
    for s, x_ref in enumerate(in_refs):
        for m in range(4):
            a_ref[s, :, BLOCK * m : BLOCK * (m + 1)] = x_ref[m, 0, 0]
            b_ref[s, :, BLOCK * m : BLOCK * (m + 1)] = x_ref[m, 0, 1]


def from_blocks(*parts):
    rows = parts[0].shape[2]
    return pl.pallas_call(
        copy_rows,
        grid=(2,),
        in_specs=[pl.BlockSpec((4, 1, 2, rows, BLOCK), lambda c: (0, c, 0, 0, 0))] * SAMPLE_COUNT,
        out_specs=[pl.BlockSpec((SAMPLE_COUNT, rows, 4 * BLOCK), lambda c: (0, 0, c))] * 2,
        out_shape=[jax.ShapeDtypeStruct((SAMPLE_COUNT, rows, 8 * BLOCK), parts[0].dtype)] * 2,
        name="from_blocks",
    )(*(x.reshape(4, 2, 2, rows, BLOCK) for x in parts))


def exchange(x):
    return lax.all_to_all(x, "tp", split_axis=0, concat_axis=0, axis_index_groups=HALVES)


def llm_hidden(llm_query, llm_kv):
    half = lax.axis_index("tp") // 8
    rows = llm_kv.shape[2]
    kv = llm_kv[0]
    keep = lax.dynamic_slice_in_dim(kv, half * 512, 512, 2)
    give = lax.dynamic_slice_in_dim(kv, (1 - half) * 512, 512, 2)
    take = lax.ppermute(give, "tp", SWAP_HALF)
    both = jnp.stack([keep, take])
    both = both.reshape(2, 2, rows, 4, HEAD_SIZE).transpose(3, 0, 1, 2, 4)
    both = jnp.broadcast_to(both[:, None], (4, 2, 2, 2, rows, HEAD_SIZE))
    got = exchange(both.reshape(8, 2, 2, rows, HEAD_SIZE))
    keys = got[:, :, 0].reshape(16 * rows, HEAD_SIZE)
    values = got[:, :, 1].reshape(16 * rows, HEAD_SIZE)
    source_half = jnp.stack([half, 1 - half])
    place = jnp.arange(8)[:, None, None] + 8 * source_half[None, :, None]
    position = (place * rows + jnp.arange(rows)[None, None, :]).reshape(1, 16 * rows)
    heads = llm_query.shape[2] // HEAD_SIZE
    queries = llm_query[0].reshape(QUERY_TOKENS * heads, HEAD_SIZE)
    scores = jnp.dot(queries, keys.T, preferred_element_type=jnp.float32) * SCALE
    token = (jnp.arange(QUERY_TOKENS * heads) // heads)[:, None]
    scores = jnp.where(position <= PROMPT + token, scores, -1e30)
    top = jnp.max(scores, axis=1, keepdims=True)
    terms = jnp.exp(scores - top)
    weights = (terms / jnp.sum(terms, axis=1, keepdims=True)).astype(jnp.bfloat16)
    mixed = jnp.dot(weights, values, preferred_element_type=jnp.float32)
    return mixed.astype(jnp.bfloat16).reshape(QUERY_TOKENS, heads * HEAD_SIZE)


def gather_run(connector):
    got = connector[None]
    for k in (4, 2, 1):
        pairs = [(8 * a + b, 8 * a + (b ^ k)) for a in range(4) for b in range(8)]
        got = jnp.concatenate([got, lax.ppermute(got, "fsdp", pairs)])
    return got


def gather_ring(hidden):
    got = [hidden]
    for k in (1, 2, 3):
        pairs = [(8 * a + b, 8 * (a ^ k) + b) for a in range(4) for b in range(8)]
        got.append(lax.ppermute(hidden, "fsdp", pairs))
    return jnp.concatenate(got)


def context_tokens(rows, columns):
    f = lax.axis_index("fsdp")
    y, zl = f // 8, f % 8
    width = columns.shape[2]
    part = jnp.einsum("rk,skn->rsn", rows, columns, preferred_element_type=jnp.float32)
    part = part.astype(jnp.bfloat16).reshape(2, 2, QUERY_TOKENS, 2, 2, 2, width)
    part = part.transpose(5, 4, 1, 0, 3, 2, 6).reshape(8, 2, 2, QUERY_TOKENS, width)
    got = exchange(part)
    mine = jnp.sum(got.astype(jnp.float32), axis=0).astype(jnp.bfloat16)
    there = lax.ppermute(mine, "tp", SWAP_HALF)
    mine = (mine.astype(jnp.float32) + there.astype(jnp.float32)).astype(jnp.bfloat16)
    got = []
    for a in range(2):
        pairs = joint(lambda y, z, h, m, c: (y ^ (2 * a + c), z, h, m ^ (z // 2), y % 2))
        got.append(lax.ppermute(mine[a], ("fsdp", "tp"), pairs))
    one, two = got
    keys = jnp.where(y < 2, one, two)
    values = jnp.where(y < 2, two, one)
    both = jnp.stack([keys, values])
    first = jnp.where(zl % 2 == 0, both[:, 0], both[:, 1])
    second = jnp.where(zl % 2 == 0, both[:, 1], both[:, 0])
    return jnp.concatenate([first, second], axis=2)


def attention_kernel(q_ref, near_ref, fk_ref, fv_ref, o_ref):
    half = LATENT_TOKENS // 2
    near_k = near_ref[:, 0].reshape(half, HEAD_SIZE)
    far_k = fk_ref[...].reshape(half, HEAD_SIZE)
    near_v = near_ref[:, 1].reshape(half, HEAD_SIZE)
    far_v = fv_ref[...].reshape(half, HEAD_SIZE)
    transposed = (((1,), (1,)), ((), ()))
    for part in range(4):
        q = q_ref[2 * part : 2 * part + 2, 0].reshape(half // 4, HEAD_SIZE)
        near = lax.dot_general(q, near_k, transposed, preferred_element_type=jnp.float32)
        far = lax.dot_general(q, far_k, transposed, preferred_element_type=jnp.float32)
        top = jnp.maximum(jnp.max(near, axis=1, keepdims=True), jnp.max(far, axis=1, keepdims=True))
        near = jnp.exp2((near - top) * (SCALE * LOG2E))
        far = jnp.exp2((far - top) * (SCALE * LOG2E))
        total = jnp.sum(near, axis=1, keepdims=True) + jnp.sum(far, axis=1, keepdims=True)
        out = jnp.dot(near.astype(jnp.bfloat16), near_v, preferred_element_type=jnp.float32)
        out += jnp.dot(far.astype(jnp.bfloat16), far_v, preferred_element_type=jnp.float32)
        out = (out / total).astype(jnp.bfloat16)
        o_ref[2 * part : 2 * part + 2] = out.reshape(2, half // 8, HEAD_SIZE)


def attention(sample, query_gradient, near, far_k, far_v):
    rows = near.shape[2]
    spec = pl.BlockSpec((8, rows, HEAD_SIZE), lambda n: (0, 0, n))
    return pl.pallas_call(
        attention_kernel,
        grid=(3,),
        in_specs=[
            pl.BlockSpec((8, 1, rows, HEAD_SIZE), lambda n: (0, sample, 0, n)),
            pl.BlockSpec((8, 2, rows, HEAD_SIZE), lambda n: (0, 0, 0, n)),
            spec,
            spec,
        ],
        out_specs=spec,
        out_shape=jax.ShapeDtypeStruct((8, rows, BLOCK), jnp.bfloat16),
        name="latent_attention",
    )(query_gradient, near, far_k, far_v)


def cross_kernel(so_ref, g_ref, context_ref, *refs):
    carry_ref = refs[0] if len(refs) == 3 else None
    out_ref, cgrad_ref = refs[-2:]
    half = LATENT_TOKENS // 2
    transposed = (((1,), (1,)), ((), ()))
    first = (((0,), (0,)), ((), ()))
    so = so_ref[...].reshape(half, HEAD_SIZE).astype(jnp.float32)
    g = g_ref[:, 0].reshape(half, HEAD_SIZE)
    ck = context_ref[0].astype(jnp.float32)
    cv = context_ref[1]
    r = lax.rsqrt(jnp.mean(so * so, axis=1, keepdims=True) + norm_eps)
    yq = so * r
    qn = yq.astype(jnp.bfloat16)
    rk = lax.rsqrt(jnp.mean(ck * ck, axis=1, keepdims=True) + norm_eps)
    yk = ck * rk
    kn = yk.astype(jnp.bfloat16)
    scores = lax.dot_general(kn, qn, transposed, preferred_element_type=jnp.float32) * SCALE
    terms = jnp.exp(scores)
    cw = terms / jnp.sum(terms, axis=0, keepdims=True)
    cb = cw.astype(jnp.bfloat16)
    cross = lax.dot_general(cb, cv, first, preferred_element_type=jnp.float32)
    out_ref[:, 0] = (so + cross).astype(jnp.bfloat16).reshape(8, half // 8, HEAD_SIZE)
    dcv = jnp.dot(cb, g, preferred_element_type=jnp.float32)
    dcw = lax.dot_general(cv, g, transposed, preferred_element_type=jnp.float32)
    delta = jnp.sum(cw * dcw, axis=0, keepdims=True)
    ds = (cw * (dcw - delta) * SCALE).astype(jnp.bfloat16)
    dqn = lax.dot_general(ds, kn, first, preferred_element_type=jnp.float32)
    dkn = jnp.dot(ds, qn, preferred_element_type=jnp.float32)
    inner = jnp.mean(dqn * yq, axis=1, keepdims=True)
    grad = g.astype(jnp.float32) + r * (dqn - yq * inner)
    out_ref[:, 1] = grad.astype(jnp.bfloat16).reshape(8, half // 8, HEAD_SIZE)
    if carry_ref is None:
        cgrad_ref[0] = dkn
        cgrad_ref[1] = dcv
    else:
        total = carry_ref[0] + dkn
        along = jnp.mean(total * yk, axis=1, keepdims=True)
        cgrad_ref[0] = (rk * (total - yk * along)).astype(jnp.bfloat16)
        cgrad_ref[1] = (carry_ref[1] + dcv).astype(jnp.bfloat16)


def cross(sample, so, query_gradient, context, carry):
    rows = so.shape[1]
    context_spec = pl.BlockSpec((2, QUERY_TOKENS, HEAD_SIZE), lambda n: (0, 0, n))
    pair_spec = pl.BlockSpec((8, 2, rows, HEAD_SIZE), lambda n: (0, 0, 0, n))
    return pl.pallas_call(
        cross_kernel,
        grid=(3,),
        in_specs=[
            pl.BlockSpec((8, rows, HEAD_SIZE), lambda n: (0, 0, n)),
            pl.BlockSpec((8, 1, rows, HEAD_SIZE), lambda n: (0, 2 + sample, 0, n)),
            context_spec,
        ]
        + [context_spec] * len(carry),
        out_specs=[pair_spec, context_spec],
        out_shape=[
            jax.ShapeDtypeStruct((8, 2, rows, BLOCK), jnp.bfloat16),
            jax.ShapeDtypeStruct(context.shape, jnp.bfloat16 if carry else jnp.float32),
        ],
        name="cross_attention",
    )(so, query_gradient, context, *carry)


def context_gradient(partial):
    half = lax.axis_index("tp") // 8
    width = BLOCK // 2
    low, high = partial[:, :, :width], partial[:, :, width:]
    first = jnp.where(half == 0, low, high)
    second = jnp.where(half == 0, high, low)
    place = lambda h, m, c: 8 * h + 2 * m + c
    coords = [(h, m, c) for h in range(2) for m in range(4) for c in range(2)]
    one = lax.ppermute(first, "tp", [(place(h, m, c), place(c, m, h)) for h, m, c in coords])
    two = lax.ppermute(second, "tp", [(place(h, m, c), place(c, m, 1 - h)) for h, m, c in coords])
    return (one.astype(jnp.float32) + two.astype(jnp.float32)).astype(jnp.bfloat16)[None]


def shards(llm_query, llm_kv, connector, self_query, self_key, latent_value, cotangent):
    return layer(llm_query, llm_kv, connector, self_query[0], self_key[0], latent_value[0], cotangent[0])


def layer(llm_query, llm_kv, connector, query, key, value, cotangent):
    swap = lambda x: lax.ppermute(x, "tp", SWAP_HALF)
    raw = swap(key[:1])
    near = [exchange(to_blocks(s, 1, key, value)) for s in range(SAMPLE_COUNT)]
    far = [[None, swap(near[0][:, 1])]]
    far.append([swap(near[1][:, i]) for i in range(2)])
    far[0][0] = exchange(to_blocks(0, 1, raw))[:, 0]
    columns = gather_run(connector)
    hidden = llm_hidden(llm_query, llm_kv)
    query_gradient = exchange(to_blocks(0, 2, query, cotangent))
    context = context_tokens(gather_ring(hidden), columns)
    out, carry = [], ()
    for s in range(SAMPLE_COUNT):
        so = attention(s, query_gradient, near[s], *far[s])
        result, partial = cross(s, so, query_gradient, context, carry)
        carry = (partial,)
        out.append(exchange(result))
    context_grad = context_gradient(partial)
    latent_out, self_grad = from_blocks(*out)
    return (latent_out[None], self_grad[None], context_grad)


def solution(mesh):
    placed = (
        P("fsdp", None, "tp"),
        P("fsdp", None, "tp", None),
        P("tp", "fsdp"),
        P("fsdp", None, "tp", None),
        P("fsdp", None, "tp", None),
        P("fsdp", None, "tp", None),
        P("fsdp", None, "tp", None),
    )
    return jax.shard_map(
        shards,
        mesh=mesh,
        in_specs=placed,
        out_specs=(
            P("fsdp", None, "tp", None),
            P("fsdp", None, "tp", None),
            P("fsdp", None, None, "tp"),
        ),
        check_vma=False,
    )
```

```python
import jax
import jax.numpy as jnp
from jax import lax
from jax.experimental import pallas as pl
from jax.sharding import PartitionSpec as P


HEAD_SIZE = 128
QUERY_TOKENS = 64
LATENT_TOKENS = 1024
SAMPLE_COUNT = 2
PROMPT = 256

SCALE = HEAD_SIZE ** (-0.5)
LOG2E = 1.4426950408889634
norm_eps = 1e-06


HALVES = [list(range(8)), list(range(8, 16))]
SWAP_HALF = [(t, (t + 8) % 16) for t in range(16)]
BLOCK = 3 * HEAD_SIZE


def joint(move):
    pairs = []
    for y in range(4):
        for zl in range(8):
            for h in range(2):
                for m in range(4):
                    for c in range(2):
                        y2, zl2, h2, m2, c2 = move(y, zl, h, m, c)
                        source = (8 * y + zl) * 16 + 8 * h + 2 * m + c
                        target = (8 * y2 + zl2) * 16 + 8 * h2 + 2 * m2 + c2
                        pairs.append((source, target))
    return pairs


def copy_blocks(*refs):
    *x_refs, o_ref = refs
    at = 0
    for x_ref in x_refs:
        count = x_ref.shape[0]
        for m in range(4):
            o_ref[m, 0, at : at + count] = x_ref[:, :, BLOCK * m : BLOCK * (m + 1)]
        at += count


def to_blocks(first, count, *parts):
    rows = parts[0].shape[1]
    total = count * len(parts)
    out = pl.pallas_call(
        copy_blocks,
        grid=(2,),
        in_specs=[pl.BlockSpec((count, rows, 4 * BLOCK), lambda c: (first, 0, c))] * len(parts),
        out_specs=pl.BlockSpec((4, 1, total, rows, BLOCK), lambda c: (0, c, 0, 0, 0)),
        out_shape=jax.ShapeDtypeStruct((4, 2, total, rows, BLOCK), parts[0].dtype),
        name="to_blocks",
    )(*parts)
    return out.reshape(8, total, rows, BLOCK)


def copy_rows(*refs):
    *in_refs, a_ref, b_ref = refs
    for s, x_ref in enumerate(in_refs):
        for m in range(4):
            a_ref[s, :, BLOCK * m : BLOCK * (m + 1)] = x_ref[m, 0, 0]
            b_ref[s, :, BLOCK * m : BLOCK * (m + 1)] = x_ref[m, 0, 1]


def from_blocks(*parts):
    rows = parts[0].shape[2]
    return pl.pallas_call(
        copy_rows,
        grid=(2,),
        in_specs=[pl.BlockSpec((4, 1, 2, rows, BLOCK), lambda c: (0, c, 0, 0, 0))] * SAMPLE_COUNT,
        out_specs=[pl.BlockSpec((SAMPLE_COUNT, rows, 4 * BLOCK), lambda c: (0, 0, c))] * 2,
        out_shape=[jax.ShapeDtypeStruct((SAMPLE_COUNT, rows, 8 * BLOCK), parts[0].dtype)] * 2,
        name="from_blocks",
    )(*(x.reshape(4, 2, 2, rows, BLOCK) for x in parts))


def exchange(x):
    return lax.all_to_all(x, "tp", split_axis=0, concat_axis=0, axis_index_groups=HALVES)


def llm_hidden(llm_query, llm_kv):
    half = lax.axis_index("tp") // 8
    rows = llm_kv.shape[2]
    kv = llm_kv[0]
    keep = lax.dynamic_slice_in_dim(kv, half * 512, 512, 2)
    give = lax.dynamic_slice_in_dim(kv, (1 - half) * 512, 512, 2)
    take = lax.ppermute(give, "tp", SWAP_HALF)
    both = jnp.stack([keep, take])
    both = both.reshape(2, 2, rows, 4, HEAD_SIZE).transpose(3, 0, 1, 2, 4)
    both = jnp.broadcast_to(both[:, None], (4, 2, 2, 2, rows, HEAD_SIZE))
    got = exchange(both.reshape(8, 2, 2, rows, HEAD_SIZE))
    keys = got[:, :, 0].reshape(16 * rows, HEAD_SIZE)
    values = got[:, :, 1].reshape(16 * rows, HEAD_SIZE)
    source_half = jnp.stack([half, 1 - half])
    place = jnp.arange(8)[:, None, None] + 8 * source_half[None, :, None]
    position = (place * rows + jnp.arange(rows)[None, None, :]).reshape(1, 16 * rows)
    heads = llm_query.shape[2] // HEAD_SIZE
    queries = llm_query[0].reshape(QUERY_TOKENS * heads, HEAD_SIZE)
    scores = jnp.dot(queries, keys.T, preferred_element_type=jnp.float32) * SCALE
    token = (jnp.arange(QUERY_TOKENS * heads) // heads)[:, None]
    scores = jnp.where(position <= PROMPT + token, scores, -1e30)
    top = jnp.max(scores, axis=1, keepdims=True)
    terms = jnp.exp(scores - top)
    weights = (terms / jnp.sum(terms, axis=1, keepdims=True)).astype(jnp.bfloat16)
    mixed = jnp.dot(weights, values, preferred_element_type=jnp.float32)
    return mixed.astype(jnp.bfloat16).reshape(QUERY_TOKENS, heads * HEAD_SIZE)


def gather_columns(connector):
    got = connector[None]
    for k in (2, 1):
        pairs = [(8 * a + b, 8 * a + (b ^ k)) for a in range(4) for b in range(8)]
        got = jnp.concatenate([got, lax.ppermute(got, "fsdp", pairs)])
    return got


def gather_rows(hidden):
    pairs = [(8 * a + b, 8 * a + (b ^ 4)) for a in range(4) for b in range(8)]
    got = [jnp.concatenate([hidden, lax.ppermute(hidden, "fsdp", pairs)])]
    for k in (1, 2, 3):
        pairs = [(8 * a + b, 8 * (a ^ k) + b) for a in range(4) for b in range(8)]
        got.append(lax.ppermute(got[0], "fsdp", pairs))
    return jnp.concatenate(got)


def context_tokens(rows, columns):
    f = lax.axis_index("fsdp")
    y, zl = f // 8, f % 8
    width = columns.shape[2]
    part = jnp.einsum("rk,skn->rsn", rows, columns, preferred_element_type=jnp.float32)
    part = part.astype(jnp.bfloat16).reshape(2, 2, 2, QUERY_TOKENS, 2, 2, width)
    part = part.transpose(2, 5, 1, 0, 4, 3, 6).reshape(8, 2, 2, QUERY_TOKENS, width)
    got = exchange(part)
    mine = jnp.sum(got.astype(jnp.float32), axis=0).astype(jnp.bfloat16)
    there = lax.ppermute(mine, "tp", SWAP_HALF)
    mine = (mine.astype(jnp.float32) + there.astype(jnp.float32)).astype(jnp.bfloat16)
    got = []
    for a in range(2):
        pairs = joint(
            lambda y, z, h, m, c: (
                y ^ (2 * a + c),
                z ^ (4 * (m // 2)),
                h,
                2 * (z // 4) + (z // 2 % 2 ^ m % 2),
                y % 2,
            )
        )
        got.append(lax.ppermute(mine[a], ("fsdp", "tp"), pairs))
    one, two = got
    keys = jnp.where(y < 2, one, two)
    values = jnp.where(y < 2, two, one)
    both = jnp.stack([keys, values])
    first = jnp.where(zl % 2 == 0, both[:, 0], both[:, 1])
    second = jnp.where(zl % 2 == 0, both[:, 1], both[:, 0])
    return jnp.concatenate([first, second], axis=2)


def attention_kernel(q_ref, near_ref, fk_ref, fv_ref, o_ref):
    half = LATENT_TOKENS // 2
    near_k = near_ref[:, 0].reshape(half, HEAD_SIZE)
    far_k = fk_ref[...].reshape(half, HEAD_SIZE)
    near_v = near_ref[:, 1].reshape(half, HEAD_SIZE)
    far_v = fv_ref[...].reshape(half, HEAD_SIZE)
    transposed = (((1,), (1,)), ((), ()))
    for part in range(4):
        q = q_ref[2 * part : 2 * part + 2, 0].reshape(half // 4, HEAD_SIZE)
        near = lax.dot_general(q, near_k, transposed, preferred_element_type=jnp.float32)
        far = lax.dot_general(q, far_k, transposed, preferred_element_type=jnp.float32)
        top = jnp.maximum(jnp.max(near, axis=1, keepdims=True), jnp.max(far, axis=1, keepdims=True))
        near = jnp.exp2((near - top) * (SCALE * LOG2E))
        far = jnp.exp2((far - top) * (SCALE * LOG2E))
        total = jnp.sum(near, axis=1, keepdims=True) + jnp.sum(far, axis=1, keepdims=True)
        out = jnp.dot(near.astype(jnp.bfloat16), near_v, preferred_element_type=jnp.float32)
        out += jnp.dot(far.astype(jnp.bfloat16), far_v, preferred_element_type=jnp.float32)
        out = (out / total).astype(jnp.bfloat16)
        o_ref[2 * part : 2 * part + 2] = out.reshape(2, half // 8, HEAD_SIZE)


def attention(sample, query_gradient, near, far_k, far_v):
    rows = near.shape[2]
    spec = pl.BlockSpec((8, rows, HEAD_SIZE), lambda n: (0, 0, n))
    return pl.pallas_call(
        attention_kernel,
        grid=(3,),
        in_specs=[
            pl.BlockSpec((8, 1, rows, HEAD_SIZE), lambda n: (0, sample, 0, n)),
            pl.BlockSpec((8, 2, rows, HEAD_SIZE), lambda n: (0, 0, 0, n)),
            spec,
            spec,
        ],
        out_specs=spec,
        out_shape=jax.ShapeDtypeStruct((8, rows, BLOCK), jnp.bfloat16),
        name="latent_attention",
    )(query_gradient, near, far_k, far_v)


def cross_kernel(so_ref, g_ref, context_ref, *refs):
    carry_ref = refs[0] if len(refs) == 3 else None
    out_ref, cgrad_ref = refs[-2:]
    half = LATENT_TOKENS // 2
    transposed = (((1,), (1,)), ((), ()))
    first = (((0,), (0,)), ((), ()))
    so = so_ref[...].reshape(half, HEAD_SIZE).astype(jnp.float32)
    g = g_ref[:, 0].reshape(half, HEAD_SIZE)
    ck = context_ref[0].astype(jnp.float32)
    cv = context_ref[1]
    r = lax.rsqrt(jnp.mean(so * so, axis=1, keepdims=True) + norm_eps)
    yq = so * r
    qn = yq.astype(jnp.bfloat16)
    rk = lax.rsqrt(jnp.mean(ck * ck, axis=1, keepdims=True) + norm_eps)
    yk = ck * rk
    kn = yk.astype(jnp.bfloat16)
    scores = lax.dot_general(kn, qn, transposed, preferred_element_type=jnp.float32) * SCALE
    terms = jnp.exp(scores)
    cw = terms / jnp.sum(terms, axis=0, keepdims=True)
    cb = cw.astype(jnp.bfloat16)
    cross = lax.dot_general(cb, cv, first, preferred_element_type=jnp.float32)
    out_ref[:, 0] = (so + cross).astype(jnp.bfloat16).reshape(8, half // 8, HEAD_SIZE)
    dcv = jnp.dot(cb, g, preferred_element_type=jnp.float32)
    dcw = lax.dot_general(cv, g, transposed, preferred_element_type=jnp.float32)
    delta = jnp.sum(cw * dcw, axis=0, keepdims=True)
    ds = (cw * (dcw - delta) * SCALE).astype(jnp.bfloat16)
    dqn = lax.dot_general(ds, kn, first, preferred_element_type=jnp.float32)
    dkn = jnp.dot(ds, qn, preferred_element_type=jnp.float32)
    inner = jnp.mean(dqn * yq, axis=1, keepdims=True)
    grad = g.astype(jnp.float32) + r * (dqn - yq * inner)
    out_ref[:, 1] = grad.astype(jnp.bfloat16).reshape(8, half // 8, HEAD_SIZE)
    if carry_ref is None:
        cgrad_ref[0] = dkn
        cgrad_ref[1] = dcv
    else:
        total = carry_ref[0] + dkn
        along = jnp.mean(total * yk, axis=1, keepdims=True)
        cgrad_ref[0] = (rk * (total - yk * along)).astype(jnp.bfloat16)
        cgrad_ref[1] = (carry_ref[1] + dcv).astype(jnp.bfloat16)


def cross(sample, so, query_gradient, context, carry):
    rows = so.shape[1]
    context_spec = pl.BlockSpec((2, QUERY_TOKENS, HEAD_SIZE), lambda n: (0, 0, n))
    pair_spec = pl.BlockSpec((8, 2, rows, HEAD_SIZE), lambda n: (0, 0, 0, n))
    return pl.pallas_call(
        cross_kernel,
        grid=(3,),
        in_specs=[
            pl.BlockSpec((8, rows, HEAD_SIZE), lambda n: (0, 0, n)),
            pl.BlockSpec((8, 1, rows, HEAD_SIZE), lambda n: (0, 2 + sample, 0, n)),
            context_spec,
        ]
        + [context_spec] * len(carry),
        out_specs=[pair_spec, context_spec],
        out_shape=[
            jax.ShapeDtypeStruct((8, 2, rows, BLOCK), jnp.bfloat16),
            jax.ShapeDtypeStruct(context.shape, jnp.bfloat16 if carry else jnp.float32),
        ],
        name="cross_attention",
    )(so, query_gradient, context, *carry)


def context_gradient(partial):
    half = lax.axis_index("tp") // 8
    width = BLOCK // 2
    low, high = partial[:, :, :width], partial[:, :, width:]
    first = jnp.where(half == 0, low, high)
    second = jnp.where(half == 0, high, low)
    place = lambda h, m, c: 8 * h + 2 * m + c
    coords = [(h, m, c) for h in range(2) for m in range(4) for c in range(2)]
    one = lax.ppermute(first, "tp", [(place(h, m, c), place(c, m, h)) for h, m, c in coords])
    two = lax.ppermute(second, "tp", [(place(h, m, c), place(c, m, 1 - h)) for h, m, c in coords])
    return (one.astype(jnp.float32) + two.astype(jnp.float32)).astype(jnp.bfloat16)[None]


def shards(llm_query, llm_kv, connector, self_query, self_key, latent_value, cotangent):
    return layer(llm_query, llm_kv, connector, self_query[0], self_key[0], latent_value[0], cotangent[0])


def layer(llm_query, llm_kv, connector, query, key, value, cotangent):
    swap = lambda x: lax.ppermute(x, "tp", SWAP_HALF)
    raw = swap(key[:1])
    near = [exchange(to_blocks(s, 1, key, value)) for s in range(SAMPLE_COUNT)]
    far = [[None, swap(near[0][:, 1])]]
    far.append([swap(near[1][:, i]) for i in range(2)])
    far[0][0] = exchange(to_blocks(0, 1, raw))[:, 0]
    columns = gather_columns(connector)
    hidden = llm_hidden(llm_query, llm_kv)
    query_gradient = exchange(to_blocks(0, 2, query, cotangent))
    context = context_tokens(gather_rows(hidden), columns)
    out, carry = [], ()
    for s in range(SAMPLE_COUNT):
        so = attention(s, query_gradient, near[s], *far[s])
        result, partial = cross(s, so, query_gradient, context, carry)
        carry = (partial,)
        out.append(exchange(result))
    context_grad = context_gradient(partial)
    latent_out, self_grad = from_blocks(*out)
    return (latent_out[None], self_grad[None], context_grad)


def solution(mesh):
    placed = (
        P("fsdp", None, "tp"),
        P("fsdp", None, "tp", None),
        P("tp", "fsdp"),
        P("fsdp", None, "tp", None),
        P("fsdp", None, "tp", None),
        P("fsdp", None, "tp", None),
        P("fsdp", None, "tp", None),
    )
    return jax.shard_map(
        shards,
        mesh=mesh,
        in_specs=placed,
        out_specs=(
            P("fsdp", None, "tp", None),
            P("fsdp", None, "tp", None),
            P("fsdp", None, None, "tp"),
        ),
        check_vma=False,
    )
```

```python
import jax
import jax.numpy as jnp
from jax import lax
from jax.experimental import pallas as pl
from jax.sharding import PartitionSpec as P


HEAD_SIZE = 128
QUERY_TOKENS = 64
LATENT_TOKENS = 1024
SAMPLE_COUNT = 2
PROMPT = 256

SCALE = HEAD_SIZE ** (-0.5)
LOG2E = 1.4426950408889634
norm_eps = 1e-06


HALVES = [list(range(8)), list(range(8, 16))]
SWAP_HALF = [(t, (t + 8) % 16) for t in range(16)]
BLOCK = 3 * HEAD_SIZE


def joint(move):
    pairs = []
    for y in range(4):
        for zl in range(8):
            for h in range(2):
                for m in range(4):
                    for c in range(2):
                        y2, zl2, h2, m2, c2 = move(y, zl, h, m, c)
                        source = (8 * y + zl) * 16 + 8 * h + 2 * m + c
                        target = (8 * y2 + zl2) * 16 + 8 * h2 + 2 * m2 + c2
                        pairs.append((source, target))
    return pairs


def copy_blocks(*refs):
    *x_refs, o_ref = refs
    at = 0
    for x_ref in x_refs:
        count = x_ref.shape[0]
        for m in range(4):
            o_ref[m, 0, at : at + count] = x_ref[:, :, BLOCK * m : BLOCK * (m + 1)]
        at += count


def to_blocks(*parts):
    rows = parts[0][0].shape[1]
    total = sum(count for _, count, _ in parts)
    specs = [pl.BlockSpec((count, rows, 4 * BLOCK), lambda c, at=at: (at, 0, c)) for _, count, at in parts]
    out = pl.pallas_call(
        copy_blocks,
        grid=(2,),
        in_specs=specs,
        out_specs=pl.BlockSpec((4, 1, total, rows, BLOCK), lambda c: (0, c, 0, 0, 0)),
        out_shape=jax.ShapeDtypeStruct((4, 2, total, rows, BLOCK), parts[0][0].dtype),
        name="to_blocks",
    )(*(x for x, _, _ in parts))
    return out.reshape(8, total, rows, BLOCK)


def copy_rows(*refs):
    *in_refs, a_ref, b_ref = refs
    for s, x_ref in enumerate(in_refs):
        for m in range(4):
            a_ref[s, :, BLOCK * m : BLOCK * (m + 1)] = x_ref[m, 0, 0]
            b_ref[s, :, BLOCK * m : BLOCK * (m + 1)] = x_ref[m, 0, 1]


def from_blocks(*parts):
    rows = parts[0].shape[2]
    return pl.pallas_call(
        copy_rows,
        grid=(2,),
        in_specs=[pl.BlockSpec((4, 1, 2, rows, BLOCK), lambda c: (0, c, 0, 0, 0))] * SAMPLE_COUNT,
        out_specs=[pl.BlockSpec((SAMPLE_COUNT, rows, 4 * BLOCK), lambda c: (0, 0, c))] * 2,
        out_shape=[jax.ShapeDtypeStruct((SAMPLE_COUNT, rows, 8 * BLOCK), parts[0].dtype)] * 2,
        name="from_blocks",
    )(*(x.reshape(4, 2, 2, rows, BLOCK) for x in parts))


def exchange(x):
    return lax.all_to_all(x, "tp", split_axis=0, concat_axis=0, axis_index_groups=HALVES)


def llm_hidden(llm_query, llm_kv):
    half = lax.axis_index("tp") // 8
    rows = llm_kv.shape[2]
    kv = llm_kv[0]
    keep = lax.dynamic_slice_in_dim(kv, half * 512, 512, 2)
    give = lax.dynamic_slice_in_dim(kv, (1 - half) * 512, 512, 2)
    take = lax.ppermute(give, "tp", SWAP_HALF)
    both = jnp.stack([keep, take])
    both = both.reshape(2, 2, rows, 4, HEAD_SIZE).transpose(3, 0, 1, 2, 4)
    both = jnp.broadcast_to(both[:, None], (4, 2, 2, 2, rows, HEAD_SIZE))
    got = exchange(both.reshape(8, 2, 2, rows, HEAD_SIZE))
    keys = got[:, :, 0].reshape(16 * rows, HEAD_SIZE)
    values = got[:, :, 1].reshape(16 * rows, HEAD_SIZE)
    source_half = jnp.stack([half, 1 - half])
    place = jnp.arange(8)[:, None, None] + 8 * source_half[None, :, None]
    position = (place * rows + jnp.arange(rows)[None, None, :]).reshape(1, 16 * rows)
    heads = llm_query.shape[2] // HEAD_SIZE
    queries = llm_query[0].reshape(QUERY_TOKENS * heads, HEAD_SIZE)
    scores = jnp.dot(queries, keys.T, preferred_element_type=jnp.float32) * SCALE
    token = (jnp.arange(QUERY_TOKENS * heads) // heads)[:, None]
    scores = jnp.where(position <= PROMPT + token, scores, -1e30)
    top = jnp.max(scores, axis=1, keepdims=True)
    terms = jnp.exp(scores - top)
    weights = (terms / jnp.sum(terms, axis=1, keepdims=True)).astype(jnp.bfloat16)
    mixed = jnp.dot(weights, values, preferred_element_type=jnp.float32)
    return mixed.astype(jnp.bfloat16).reshape(QUERY_TOKENS, heads * HEAD_SIZE)


def gather_columns(connector):
    got = connector[None]
    for k in (2, 1):
        pairs = [(8 * a + b, 8 * a + (b ^ k)) for a in range(4) for b in range(8)]
        got = jnp.concatenate([got, lax.ppermute(got, "fsdp", pairs)])
    return got


def gather_rows(hidden):
    pairs = [(8 * a + b, 8 * a + (b ^ 4)) for a in range(4) for b in range(8)]
    got = [jnp.concatenate([hidden, lax.ppermute(hidden, "fsdp", pairs)])]
    for k in (1, 2, 3):
        pairs = [(8 * a + b, 8 * (a ^ k) + b) for a in range(4) for b in range(8)]
        got.append(lax.ppermute(got[0], "fsdp", pairs))
    return jnp.concatenate(got)


def context_tokens(rows, columns):
    f = lax.axis_index("fsdp")
    y, zl = f // 8, f % 8
    width = columns.shape[2]
    part = jnp.einsum("rk,skn->rsn", rows, columns, preferred_element_type=jnp.float32)
    part = part.astype(jnp.bfloat16).reshape(2, 2, 2, QUERY_TOKENS, 2, 2, width)
    part = part.transpose(2, 5, 1, 0, 4, 3, 6).reshape(8, 2, 2, QUERY_TOKENS, width)
    got = exchange(part)
    mine = jnp.sum(got.astype(jnp.float32), axis=0).astype(jnp.bfloat16)
    there = lax.ppermute(mine, "tp", SWAP_HALF)
    mine = (mine.astype(jnp.float32) + there.astype(jnp.float32)).astype(jnp.bfloat16)
    got = []
    for a in range(2):
        pairs = joint(
            lambda y, z, h, m, c: (
                y ^ (2 * a + c),
                z ^ (4 * (m // 2)),
                h,
                2 * (z // 4) + (z // 2 % 2 ^ m % 2),
                y % 2,
            )
        )
        got.append(lax.ppermute(mine[a], ("fsdp", "tp"), pairs))
    one, two = got
    keys = jnp.where(y < 2, one, two)
    values = jnp.where(y < 2, two, one)
    both = jnp.stack([keys, values])
    first = jnp.where(zl % 2 == 0, both[:, 0], both[:, 1])
    second = jnp.where(zl % 2 == 0, both[:, 1], both[:, 0])
    return jnp.concatenate([first, second], axis=2)


def attention_kernel(q_ref, near_ref, fk_ref, fv_ref, o_ref):
    half = LATENT_TOKENS // 2
    near_k = near_ref[:, 0].reshape(half, HEAD_SIZE)
    far_k = fk_ref[...].reshape(half, HEAD_SIZE)
    near_v = near_ref[:, 1].reshape(half, HEAD_SIZE)
    far_v = fv_ref[...].reshape(half, HEAD_SIZE)
    transposed = (((1,), (1,)), ((), ()))
    for part in range(4):
        q = q_ref[2 * part : 2 * part + 2, 0].reshape(half // 4, HEAD_SIZE)
        near = lax.dot_general(q, near_k, transposed, preferred_element_type=jnp.float32)
        far = lax.dot_general(q, far_k, transposed, preferred_element_type=jnp.float32)
        top = jnp.maximum(jnp.max(near, axis=1, keepdims=True), jnp.max(far, axis=1, keepdims=True))
        near = jnp.exp2((near - top) * (SCALE * LOG2E))
        far = jnp.exp2((far - top) * (SCALE * LOG2E))
        total = jnp.sum(near, axis=1, keepdims=True) + jnp.sum(far, axis=1, keepdims=True)
        out = jnp.dot(near.astype(jnp.bfloat16), near_v, preferred_element_type=jnp.float32)
        out += jnp.dot(far.astype(jnp.bfloat16), far_v, preferred_element_type=jnp.float32)
        out = (out / total).astype(jnp.bfloat16)
        o_ref[2 * part : 2 * part + 2] = out.reshape(2, half // 8, HEAD_SIZE)


def attention(sample, query_gradient, near, far_k, far_v):
    far_k, place = far_k
    rows = near.shape[2]
    spec = pl.BlockSpec((8, rows, HEAD_SIZE), lambda n: (0, 0, n))
    return pl.pallas_call(
        attention_kernel,
        grid=(3,),
        in_specs=[
            pl.BlockSpec((8, 1, rows, HEAD_SIZE), lambda n: (0, sample, 0, n)),
            pl.BlockSpec((8, 2, rows, HEAD_SIZE), lambda n: (0, 0, 0, n)),
            pl.BlockSpec((8, None, rows, HEAD_SIZE), lambda n: (0, place, 0, n)),
            spec,
        ],
        out_specs=spec,
        out_shape=jax.ShapeDtypeStruct((8, rows, BLOCK), jnp.bfloat16),
        name="latent_attention",
    )(query_gradient, near, far_k, far_v)


def cross_kernel(so_ref, g_ref, context_ref, *refs):
    carry_ref = refs[0] if len(refs) == 3 else None
    out_ref, cgrad_ref = refs[-2:]
    half = LATENT_TOKENS // 2
    transposed = (((1,), (1,)), ((), ()))
    first = (((0,), (0,)), ((), ()))
    so = so_ref[...].reshape(half, HEAD_SIZE).astype(jnp.float32)
    g = g_ref[:, 0].reshape(half, HEAD_SIZE)
    ck = context_ref[0].astype(jnp.float32)
    cv = context_ref[1]
    r = lax.rsqrt(jnp.mean(so * so, axis=1, keepdims=True) + norm_eps)
    yq = so * r
    qn = yq.astype(jnp.bfloat16)
    rk = lax.rsqrt(jnp.mean(ck * ck, axis=1, keepdims=True) + norm_eps)
    yk = ck * rk
    kn = yk.astype(jnp.bfloat16)
    scores = lax.dot_general(kn, qn, transposed, preferred_element_type=jnp.float32) * SCALE
    terms = jnp.exp(scores)
    cw = terms / jnp.sum(terms, axis=0, keepdims=True)
    cb = cw.astype(jnp.bfloat16)
    cross = lax.dot_general(cb, cv, first, preferred_element_type=jnp.float32)
    out_ref[:, 0] = (so + cross).astype(jnp.bfloat16).reshape(8, half // 8, HEAD_SIZE)
    dcv = jnp.dot(cb, g, preferred_element_type=jnp.float32)
    dcw = lax.dot_general(cv, g, transposed, preferred_element_type=jnp.float32)
    delta = jnp.sum(cw * dcw, axis=0, keepdims=True)
    ds = (cw * (dcw - delta) * SCALE).astype(jnp.bfloat16)
    dqn = lax.dot_general(ds, kn, first, preferred_element_type=jnp.float32)
    dkn = jnp.dot(ds, qn, preferred_element_type=jnp.float32)
    inner = jnp.mean(dqn * yq, axis=1, keepdims=True)
    grad = g.astype(jnp.float32) + r * (dqn - yq * inner)
    out_ref[:, 1] = grad.astype(jnp.bfloat16).reshape(8, half // 8, HEAD_SIZE)
    if carry_ref is None:
        cgrad_ref[0] = dkn
        cgrad_ref[1] = dcv
    else:
        total = carry_ref[0] + dkn
        along = jnp.mean(total * yk, axis=1, keepdims=True)
        cgrad_ref[0] = (rk * (total - yk * along)).astype(jnp.bfloat16)
        cgrad_ref[1] = (carry_ref[1] + dcv).astype(jnp.bfloat16)


def cross(sample, so, query_gradient, context, carry):
    rows = so.shape[1]
    context_spec = pl.BlockSpec((2, QUERY_TOKENS, HEAD_SIZE), lambda n: (0, 0, n))
    pair_spec = pl.BlockSpec((8, 2, rows, HEAD_SIZE), lambda n: (0, 0, 0, n))
    return pl.pallas_call(
        cross_kernel,
        grid=(3,),
        in_specs=[
            pl.BlockSpec((8, rows, HEAD_SIZE), lambda n: (0, 0, n)),
            pl.BlockSpec((8, 1, rows, HEAD_SIZE), lambda n: (0, 2 + sample, 0, n)),
            context_spec,
        ]
        + [context_spec] * len(carry),
        out_specs=[pair_spec, context_spec],
        out_shape=[
            jax.ShapeDtypeStruct((8, 2, rows, BLOCK), jnp.bfloat16),
            jax.ShapeDtypeStruct(context.shape, jnp.bfloat16 if carry else jnp.float32),
        ],
        name="cross_attention",
    )(so, query_gradient, context, *carry)


def context_gradient(partial):
    half = lax.axis_index("tp") // 8
    width = BLOCK // 2
    low, high = partial[:, :, :width], partial[:, :, width:]
    first = jnp.where(half == 0, low, high)
    second = jnp.where(half == 0, high, low)
    place = lambda h, m, c: 8 * h + 2 * m + c
    coords = [(h, m, c) for h in range(2) for m in range(4) for c in range(2)]
    one = lax.ppermute(first, "tp", [(place(h, m, c), place(c, m, h)) for h, m, c in coords])
    two = lax.ppermute(second, "tp", [(place(h, m, c), place(c, m, 1 - h)) for h, m, c in coords])
    return (one.astype(jnp.float32) + two.astype(jnp.float32)).astype(jnp.bfloat16)[None]


def shards(llm_query, llm_kv, connector, self_query, self_key, latent_value, cotangent):
    return layer(llm_query, llm_kv, connector, self_query[0], self_key[0], latent_value[0], cotangent[0])


def layer(llm_query, llm_kv, connector, query, key, value, cotangent):
    swap = lambda x: lax.ppermute(x, "tp", SWAP_HALF)
    raw = swap(key[:1])
    near = [exchange(to_blocks((key, 1, s), (value, 1, s))) for s in range(SAMPLE_COUNT)]
    far_values = [swap(near[s][:, 1]) for s in range(SAMPLE_COUNT)]
    far_keys = swap(near[1][:, :1])
    columns = gather_columns(connector)
    hidden = llm_hidden(llm_query, llm_kv)
    query_gradient = exchange(to_blocks((query, 2, 0), (cotangent, 2, 0), (raw, 1, 0)))
    far_keys = [(query_gradient, 4), (far_keys, 0)]
    context = context_tokens(gather_rows(hidden), columns)
    out, carry = [], ()
    for s in range(SAMPLE_COUNT):
        so = attention(s, query_gradient, near[s], far_keys[s], far_values[s])
        result, partial = cross(s, so, query_gradient, context, carry)
        carry = (partial,)
        out.append(exchange(result))
    context_grad = context_gradient(partial)
    latent_out, self_grad = from_blocks(*out)
    return (latent_out[None], self_grad[None], context_grad)


def solution(mesh):
    placed = (
        P("fsdp", None, "tp"),
        P("fsdp", None, "tp", None),
        P("tp", "fsdp"),
        P("fsdp", None, "tp", None),
        P("fsdp", None, "tp", None),
        P("fsdp", None, "tp", None),
        P("fsdp", None, "tp", None),
    )
    return jax.shard_map(
        shards,
        mesh=mesh,
        in_specs=placed,
        out_specs=(
            P("fsdp", None, "tp", None),
            P("fsdp", None, "tp", None),
            P("fsdp", None, None, "tp"),
        ),
        check_vma=False,
    )
```
